32 devices in a mesh: span: 4 (over z), mp: 4 (over x, core), phase: 2 (over y).
Axes of the slice: x: 2, y: 2, z: 4, core: 2. Of those that a mesh axis runs over, the one named last changes fastest.
Arguments:
- latents: bfloat16 [4096, 2560], P(('span', 'phase')), may hold values from -6 to 6
- w_qkv: bfloat16 [2560, 3, 1536], P(None, None, 'mp'), may hold values from -0.125 to 0.125
- w_out: bfloat16 [1536, 2560], P('mp'), may hold values from -0.15625 to 0.15625
- decay: float32 [4, 2, 12], P('span', None, 'mp'), may hold values from 0.4 to 0.999, as said below
- frame_ids: int32 [4, 1024], P('span'), may hold values from 0 to 15, never falling along the last dimension, each value on 1 to 256 neighbouring positions
- memory_mask: int32 [4, 17], P('span'), may hold values 0 or 1
Outputs:
- refined: bfloat16 [4096, 2560], P(('span', 'phase'), 'mp')
The draws below stay inside these ranges and needn't reach their ends.
Inputs may be any that keep to these rules, and one draw needn't show every extreme that they name: `frame_ids`: along each span's 1024 tokens the frame numbers never fall, and every frame from 0 on holds 1 to 256 tokens. `decay`: every entry lies strictly between 0 and 1.
All inputs are finite; a program needn't handle non-finite values. No bound on the sum of `memory_mask` on one device may be relied on, other than what follows from the above.
Results may differ from the reference program's by a relative error of at most 0.004.
Values may be sent and summed in bfloat16 or wider, within the bound.
A program may use at most 128 MiB of HBM per device.

```python
import math
import jax
import jax.numpy as jnp
import numpy as np
from jax import lax

D = 2560
ATTENTION_HEADS = 12
HD = 128
WIN = 64
MEM = 256
ROWS = 512
SPANS = 4
SPLIT = 2
SPAN_HALVES = 8
SPAN_LEN = 1024
TOKENS = 4096
CWIN = 17
FRAMES = 16
FRAME_MOST = 256
HC = 1536
N_MP = 4


def draw_latents(key, part):
    key_shared, key_own = jax.random.split(key)
    shared = jax.random.normal(key_shared, (SPAN_LEN, D), jnp.float32)
    own = jax.random.normal(key_own, (SPANS, SPAN_LEN, D), jnp.float32)
    mixed = 0.75 * shared[None, :, :] + 0.65 * own
    mixed = jnp.clip(mixed, -6.0, 6.0)
    return mixed.reshape(TOKENS, D).astype(jnp.bfloat16)


def draw_decay(key, part):
    key_pick, key_spread, key_location, key_length, key_fast = jax.random.split(key, 5)
    slow_share = 5
    slow = jax.random.randint(key_pick, (ATTENTION_HEADS,), 0, 10) < slow_share
    spread = jax.random.uniform(key_spread, (SPAN_HALVES, ATTENTION_HEADS), jnp.float32, 0.5, 1.0)
    gradual_decay_rate = jnp.exp(-math.log(10.0) / (3.0 * SPAN_HALVES) * spread)
    surge_location = jax.random.randint(key_location, (2,), 0, SPAN_HALVES)
    token_location = jnp.arange(SPAN_HALVES)
    removed_mask = jnp.any(token_location[:, None] == surge_location[None, :], axis=1)
    surge_length = jax.random.uniform(key_length, (SPAN_HALVES, ATTENTION_HEADS), jnp.float32, 0.5, 0.8)
    gradual_decay_rate = jnp.where(removed_mask[:, None], gradual_decay_rate * surge_length, gradual_decay_rate)
    fast_rate = jax.random.uniform(key_fast, (SPAN_HALVES, ATTENTION_HEADS), jnp.float32, 0.55, 0.85)
    rate = jnp.where(slow[None, :], gradual_decay_rate, fast_rate)
    return rate.reshape(SPANS, SPLIT, ATTENTION_HEADS).astype(jnp.float32)


def with_ends(values, key, low, largest):
    longest = values.shape.index(max(values.shape))
    spots = []
    for shift in (0, 1):
        where = [jax.random.randint(jax.random.fold_in(key, axis), (), 0, length) for axis, length in enumerate(values.shape)]
        where[longest] = (where[longest] + shift) % values.shape[longest]
        spots.append(tuple(where))
    return values.at[spots[0]].set(low).at[spots[1]].set(largest)


def levels(own_key, dims, pieces, least, largest):
    def one(position, blocks):
        heights = jax.random.uniform(jax.random.fold_in(jax.random.fold_in(own_key, 6), position), (blocks,), jnp.float32, least / len(pieces), largest / len(pieces))
        return jnp.repeat(jnp.exp(heights), dims[position] // blocks).reshape((-1,) + (1,) * (len(dims) - position - 1))

    factor_of = one(*pieces[0])
    for cut in pieces[1:]:
        factor_of = factor_of * one(*cut)
    return factor_of


def length_profile(amount, total, limit, slope):
    loads = [(1 << 20) // math.isqrt(rank ** slope) + 1 for rank in range(2, amount + 1)]
    rest, holding = total - limit - (amount - 1), [1] * (amount - 1)
    while rest > 0:
        movable = [i for i in range(amount - 1) if holding[i] < limit]
        mass, budget = sum([loads[i] for i in movable]), rest
        for i in movable:
            more = min(limit - holding[i], max(1, budget * loads[i] // mass), rest)
            holding[i] = holding[i] + more
            rest = rest - more
    return np.array([limit] + holding)


def ragged_sizes(stream_key, count, total, most, skew):
    if count == 2:
        one = jax.random.randint(stream_key, (), max(1, total - most), min(most, total - 1) + 1)
        return jnp.stack([one, total - one])
    lengths = jnp.asarray(length_profile(count, total, most, skew), jnp.int32)
    couples = (count - 1) // 2
    source_of, sink = lengths[1:1 + 2 * couples:2], lengths[2:2 + 2 * couples:2]
    room = jnp.minimum(source_of - 1, most - sink)
    passed = jax.random.randint(jax.random.fold_in(stream_key, 1), (couples,), 0, 1 << 20) % (room + 1)
    lengths = lengths.at[1:1 + 2 * couples:2].set(source_of - passed).at[2:2 + 2 * couples:2].set(sink + passed)
    return lengths[jax.random.permutation(jax.random.fold_in(stream_key, 2), count)]


def bell_draw(key, shape, scale, bound, pieces=(), kind=jnp.bfloat16):
    gain = levels(key, shape, pieces, -0.22, 0.18) if pieces else 1.0
    drawn = jax.random.normal(key, shape, jnp.float32) * scale * gain
    return jnp.minimum(jnp.maximum(drawn, -bound), bound).astype(kind)


def setup_inputs(seed: int = 0) -> dict:
    splits = jax.random.split(jax.random.key(seed), 7)
    return {
        "latents": draw_latents(jax.random.fold_in(splits[6], 71), 0),
        "w_qkv": bell_draw(splits[1], (D, 3, HC), D ** -0.5, 0.125, ((2, 4),)),
        "w_out": bell_draw(splits[2], (HC, D), HC ** -0.5, 0.15625, ((0, 4),)),
        "decay": draw_decay(jax.random.fold_in(splits[6], 71), 0),
        "frame_ids": jax.vmap(lambda own: jnp.searchsorted(jnp.cumsum(ragged_sizes(own, FRAMES, SPAN_LEN, FRAME_MOST, 1)), jnp.arange(SPAN_LEN), side="right"))(jax.random.split(splits[4], SPANS)).reshape((SPANS, SPAN_LEN)).astype(jnp.int32),
        "memory_mask": with_ends((jax.random.randint(splits[5], (SPANS, CWIN), 0, 4) < 3).astype(jnp.int32), jax.random.fold_in(splits[5], 1), 0, 1),
    }


outside_frame = 1048576
epsilon = 1e-06

def head_normed(raw):
    count = raw.shape[0]
    grouped = raw.reshape(count, -1, HD)
    scaled = grouped * lax.rsqrt(lax.optimization_barrier(jnp.mean(grouped * grouped, axis=-1, keepdims=True)) + epsilon)
    return scaled.reshape(count, -1).astype(jnp.bfloat16)

def project_span(rows_in, w_qkv):
    mixed = jnp.dot(rows_in, w_qkv.reshape(D, 3 * HC), preferred_element_type=jnp.float32)
    return (head_normed(mixed[:, :HC]), head_normed(mixed[:, HC:2 * HC]), mixed[:, 2 * HC:].astype(jnp.bfloat16))

def window_attend(queries_pad, keys_ext, values_ext, frames_ext, memory_keys, memory_values, memory_open):
    total_rows, width = queries_pad.shape
    heads = width // HD
    count = total_rows // WIN
    score_scale = HD ** (-0.5)
    window_query = queries_pad.astype(jnp.float32).reshape(count, WIN, heads, HD)
    key_win = keys_ext.astype(jnp.float32).reshape(count, WIN, heads, HD)
    value_win = values_ext.astype(jnp.float32).reshape(count, WIN, heads, HD)
    memory_key_rows = memory_keys.astype(jnp.float32).reshape(MEM, heads, HD)
    memory_value_rows = memory_values.astype(jnp.float32).reshape(MEM, heads, HD)
    score_win = jnp.einsum('wqhd,wkhd->whqk', window_query, key_win) * score_scale
    memory_score = jnp.einsum('bntu,atu->btna', window_query, memory_key_rows) * score_scale
    frame_win = frames_ext.reshape(count, WIN)
    allowed = frame_win[:, None, None, :] <= frame_win[:, None, :, None]
    exp_win = jnp.where(allowed, jnp.exp(score_win), 0.0)
    exp_mem = jnp.where((memory_open == 1)[:, None, None, None], jnp.exp(memory_score), 0.0)
    denom = lax.optimization_barrier(jnp.sum(exp_win, axis=-1, keepdims=True)) + lax.optimization_barrier(jnp.sum(exp_mem, axis=-1, keepdims=True))
    weight_win = lax.optimization_barrier((exp_win / denom).astype(jnp.bfloat16))
    memory_weight = lax.optimization_barrier((exp_mem / denom).astype(jnp.bfloat16))
    refined_output = jnp.einsum('whqk,wkhd->wqhd', weight_win.astype(jnp.float32), value_win)
    refined_output = refined_output + jnp.einsum('bykl,lyp->bkyp', memory_weight.astype(jnp.float32), memory_value_rows)
    return refined_output.reshape(total_rows, width).astype(jnp.bfloat16)

def reference(latents, w_qkv, w_out, decay, frame_ids, memory_mask):
    spanned = latents.reshape(SPANS, SPAN_LEN, D)
    queries_all, keys_all, values_all = lax.map(lambda block: project_span(block, w_qkv), spanned)
    rates = jnp.repeat(decay.reshape(SPAN_HALVES, ATTENTION_HEADS), HD, axis=1)
    last_keys = keys_all.reshape(SPAN_HALVES, ROWS, HC)[:, ROWS - MEM:]
    last_values = values_all.reshape(SPAN_HALVES, ROWS, HC)[:, ROWS - MEM:]

    def carry_step(state, inputs):
        rate, tail_keys, tail_values = inputs
        new_keys = rate * state[0] + (1.0 - rate) * tail_keys.astype(jnp.float32)
        new_values = rate * state[1] + jnp.sqrt(1.0 - rate * rate) * tail_values.astype(jnp.float32)
        return ((new_keys, new_values), state)
    start = (jnp.zeros((MEM, HC), jnp.float32), jnp.zeros((MEM, HC), jnp.float32))
    unused, memories = lax.scan(carry_step, start, (rates, last_keys, last_values))
    memory_keys_all = memories[0].reshape(SPANS, SPLIT, MEM, HC)
    memory_values_all = memories[1].reshape(SPANS, SPLIT, MEM, HC)
    half_win = WIN // 2
    group_cols = HC // N_MP

    def finish_span(items):
        block, queries, keys, values, frames, opened, mem_keys, mem_values = items
        keys_pad = jnp.pad(keys, ((half_win, half_win), (0, 0)))
        values_pad = jnp.pad(values, ((half_win, half_win), (0, 0)))
        frames_pad = jnp.pad(frames, (half_win, half_win), constant_values=outside_frame)
        outputs = []
        for half in range(SPLIT):
            offset = half * ROWS
            queries_pad = jnp.pad(queries[offset:offset + ROWS], ((half_win, half_win), (0, 0)))
            window_start = half * (ROWS // WIN)
            memory_keys_b = lax.optimization_barrier(mem_keys[half].astype(jnp.bfloat16))
            memory_values_b = lax.optimization_barrier(mem_values[half].astype(jnp.bfloat16))
            attended = window_attend(queries_pad, keys_pad[offset:offset + ROWS + WIN], values_pad[offset:offset + ROWS + WIN], frames_pad[offset:offset + ROWS + WIN], memory_keys_b, memory_values_b, opened[window_start:window_start + ROWS // WIN + 1])[half_win:half_win + ROWS]
            total = block[offset:offset + ROWS].astype(jnp.float32)
            for group in range(N_MP):
                lower = group * group_cols
                partial_sum = jnp.dot(attended[:, lower:lower + group_cols], w_out[lower:lower + group_cols], preferred_element_type=jnp.float32).astype(jnp.bfloat16)
                partial_sum = lax.optimization_barrier(partial_sum)
                total = total + partial_sum.astype(jnp.float32)
            outputs.append(total.astype(jnp.bfloat16))
        return jnp.concatenate(outputs, axis=0)
    refined = lax.map(finish_span, (spanned, queries_all, keys_all, values_all, frame_ids, memory_mask, memory_keys_all, memory_values_all))
    return refined.reshape(TOKENS, D)
```

```python
import functools
import math

import jax
import jax.numpy as jnp
from jax import lax
from jax.experimental import pallas as pl
from jax.experimental.pallas import tpu as pltpu
from jax.sharding import PartitionSpec as P

HD = 128
WIN = 64
MEM = 256
HALF = WIN // 2
GROUP = 128
PIECES = 8
EARLY = 2
MESH = pl.DeviceIdType.MESH

outside_frame = 1048576
epsilon = 1e-06
score_factor = HD ** (-0.5) * math.log2(math.e)


def remote(src, dst, send, recv, where):
    return pltpu.make_async_remote_copy(
        src_ref=src, dst_ref=dst, send_sem=send, recv_sem=recv,
        device_id=where, device_id_type=MESH,
    )


def body(
    sizes, x_hbm, w_hbm, wo_hbm, decay_hbm, frames_hbm, opened_hbm, out,
    decay, frames, opened, x, w, wo, kv, q, num, den, att, fr, tail_in, s_in, s_out, m_out, mem,
    load_sem, ws_send, ws_recv, wo_send, wo_recv, wm_send, wm_recv, wr_send, wr_recv, y_send, y_recv, z_send, z_recv, m_send, m_recv,
    h_send, h_recv, a_send, a_recv, c_send, c_recv, r_send, r_recv,
):
    n_span, n_mp, rows, width, cols = sizes
    heads = cols // HD
    share = width // n_mp
    groups = kv.shape[1] // GROUP
    c = lax.axis_index("span")
    me = lax.axis_index("mp")
    phase = lax.axis_index("phase")
    is0 = phase == 0
    other = 1 - phase
    kept, sent = phase, 1 - phase
    sib = me + 1 - 2 * (me % 2)
    chips = n_mp // 2
    tail0 = HALF + rows - MEM
    piece = MEM // PIECES

    def load(i, src, dst):
        copy = pltpu.make_async_copy(src, dst, load_sem.at[i])
        copy.start()
        return copy

    top = rows - MEM
    x_tail = load(0, x_hbm.at[pl.ds(top, MEM)], x.at[pl.ds(top, MEM)])
    w_sent = load(1, w_hbm.at[1 + sent], w.at[:, pl.ds(0, cols)])
    w_kept = load(2, w_hbm.at[1 + kept], w.at[:, pl.ds(cols, cols)])
    x_head = load(3, x_hbm.at[pl.ds(0, top)], x.at[pl.ds(0, top)])
    w_query = load(4, w_hbm.at[0], w.at[:, pl.ds(2 * cols, cols)])
    wo_own = load(5, wo_hbm.at[:, pl.ds(pl.multiple_of(me * share, HD), share)], wo.at[me])

    small = [load(6, decay_hbm, decay), load(7, frames_hbm, frames), load(8, opened_hbm, opened)]

    barrier = pltpu.get_barrier_semaphore()
    for o in range(1, n_mp):
        pl.semaphore_signal(barrier, inc=1, device_id={"mp": (me + o) % n_mp}, device_id_type=MESH)
    pl.semaphore_signal(barrier, inc=1, device_id={"phase": other}, device_id_type=MESH)

    @pl.when(c > 0)
    def _():
        pl.semaphore_signal(barrier, inc=1, device_id={"span": c - 1}, device_id_type=MESH)

    @pl.when(c < n_span - 1)
    def _():
        pl.semaphore_signal(barrier, inc=1, device_id={"span": c + 1}, device_id_type=MESH)

    pl.semaphore_wait(barrier, n_mp + 1 + (c + n_span - 1) // n_span - (c + 1) // n_span)

    part = cols // 3 // HALF * HALF
    middle = cols - 2 * part
    my_part = pl.ds(pl.multiple_of(phase * (part + middle), HALF), part)
    middle_part = pl.ds(part, middle)

    def columns_of(m):
        return pl.ds(pl.multiple_of(m * share, HD), share)

    wo_side = remote(wo_hbm.at[:, columns_of(sib)], wo.at[me], ws_send, ws_recv, {"mp": sib})
    wo_copies, wo_relays, wo_middles = [], [], []
    for o in range(1, chips):
        for i, near in enumerate((me, sib)):
            to, source = (near + 2 * o) % n_mp, (near + n_mp - 2 * o) % n_mp
            at = 2 * (o - 1) + i
            wo_copies.append(remote(
                wo_hbm.at[my_part, columns_of(to)], wo.at[me, my_part],
                wo_send.at[at], wo_recv.at[at], {"mp": to},
            ))
            wo_middles.append(remote(
                wo_hbm.at[middle_part, columns_of(to)], wo.at[me, middle_part],
                wm_send.at[at], wm_recv.at[at], {"mp": to},
            ))
            wo_relays.append(remote(
                wo.at[source, my_part], wo.at[source, my_part],
                wr_send.at[at], wr_recv.at[at], {"phase": other},
            ))
    for copy in wo_copies + wo_middles:
        copy.start()
    wo_side.start()

    def unit(raw, flag):
        parts = []
        for i in range(heads):
            part = raw[:, i * HD:(i + 1) * HD]
            scale = lax.rsqrt(jnp.mean(part * part, axis=-1, keepdims=True) + epsilon)
            if flag is not None:
                scale = jnp.where(flag, scale, 1.0)
            parts.append((part * scale).astype(jnp.bfloat16))
        return jnp.concatenate(parts, axis=1)

    def project(first, count, column):
        return jnp.dot(
            x[first:first + count, :], w[:, column:column + cols],
            preferred_element_type=jnp.float32,
        )

    zero_rows = kv.shape[1] - (HALF + rows + HALF)
    kv[:, HALF + rows + HALF:, :] = jnp.zeros((2, zero_rows, cols), jnp.bfloat16)
    q[HALF + rows:, :] = jnp.zeros((q.shape[0] - HALF - rows, cols), jnp.bfloat16)
    q[:HALF, :] = jnp.zeros((HALF, cols), jnp.bfloat16)
    blank = pl.multiple_of(phase * (HALF + rows), HALF)
    kv[:, pl.ds(blank, HALF), :] = jnp.zeros((2, HALF, cols), jnp.bfloat16)

    @pl.when(c == 0)
    def _():
        s_in[...] = jnp.zeros(s_in.shape, s_in.dtype)

    x_tail.wait()
    w_sent.wait()
    for copy in small:
        copy.wait()
    kv[sent, tail0:tail0 + MEM, :] = unit(project(top, MEM, 0), sent == 0)
    tails, chain, moved = [], [], []
    for k in range(PIECES):
        at = pl.ds(k * piece, piece)
        copy = remote(
            kv.at[sent, pl.ds(tail0 + k * piece, piece)], tail_in.at[at],
            y_send.at[k], y_recv.at[k], {"phase": other},
        )
        copy.start()
        tails.append(copy)
        chain.append(remote(s_out.at[at], s_in.at[at], z_send.at[k], z_recv.at[k], {"span": (c + 1) % n_span}))
        moved.append(remote(m_out.at[at], mem.at[kept, at], m_send.at[k], m_recv.at[k], {"phase": other}))
    w_kept.wait()
    kv[kept, tail0:tail0 + MEM, :] = unit(project(top, MEM, cols), kept == 0)
    x_head.wait()
    kv[sent, HALF:HALF + top, :] = unit(project(0, top, 0), sent == 0)
    kv[kept, HALF:HALF + top, :] = unit(project(0, top, cols), kept == 0)
    halo_from = pl.multiple_of(HALF + other * (rows - HALF), HALF)
    halo = remote(
        kv.at[:, pl.ds(halo_from, HALF)], kv.at[:, pl.ds(blank, HALF)],
        h_send, h_recv, {"phase": other},
    )
    halo.start()

    def row_of(half):
        return jnp.concatenate(
            [jnp.broadcast_to(decay[half:half + 1, i:i + 1], (1, HD)) for i in range(heads)], axis=1
        )

    r0, r1 = row_of(0), row_of(1)

    def mix(rate):
        return jnp.where(is0, 1.0 - rate, jnp.sqrt(1.0 - rate * rate))

    f0, f1, both = mix(r0), mix(r1), r0 * r1

    def chain_piece(k):
        at = slice(k * piece, (k + 1) * piece)
        own = kv[kept, tail0 + k * piece:tail0 + (k + 1) * piece, :].astype(jnp.float32)
        tails[k].wait_recv()
        theirs = tail_in[at, :].astype(jnp.float32)
        low = f0 * jnp.where(is0, own, theirs)
        high = r1 * low + f1 * jnp.where(is0, theirs, own)

        @pl.when(c > 0)
        def _():
            chain[k].wait_recv()

        state = s_in[at, :].astype(jnp.float32)
        s_out[at, :] = (both * state + high).astype(jnp.bfloat16)

        @pl.when(c < n_span - 1)
        def _():
            chain[k].start()

        later = r0 * state + low
        m_out[at, :] = jnp.where(is0, later, state).astype(jnp.bfloat16)
        moved[k].start()
        mem[kept, at, :] = jnp.where(is0, state, later).astype(jnp.bfloat16)

    def queries():
        w_query.wait()
        for first in (0, top):
            count = top if first == 0 else rows - top
            q[HALF + first:HALF + first + count, :] = unit(project(first, count, 2 * cols), None)

    def frame_rows():
        total = frames.shape[1]
        wide = jnp.broadcast_to(frames[...], (8, total))
        ahead = pltpu.roll(wide, HALF, 1)
        behind = pltpu.roll(wide, total - (rows - HALF), 1)
        place = lax.broadcasted_iota(jnp.int32, wide.shape, 1)
        ext = jnp.where(is0, ahead, behind)
        least = jnp.where(is0, HALF, 0)
        limit = jnp.where(is0, total + HALF, rows + HALF)
        ext = jnp.where((place >= least) & (place < limit), ext, outside_frame)
        for g in range(groups):
            fr[g] = ext[:, g * GROUP:(g + 1) * GROUP].astype(jnp.float32)

    def local_group(g, carry):
        base = g * GROUP
        key_frame = jnp.broadcast_to(fr[g][0:1, :], (GROUP, GROUP))
        same = (
            lax.broadcasted_iota(jnp.int32, (GROUP, GROUP), 0) // WIN
            == lax.broadcasted_iota(jnp.int32, (GROUP, GROUP), 1) // WIN
        )
        allowed = same & (key_frame <= key_frame.T)
        spans = [slice(i * HD, (i + 1) * HD) for i in range(heads)]
        scores = [
            lax.dot_general(
                q[pl.ds(base, GROUP), span_of], kv[0, pl.ds(base, GROUP), span_of],
                (((1,), (1,)), ((), ())), preferred_element_type=jnp.float32,
            )
            for span_of in spans
        ]
        weights = [jnp.where(allowed, jnp.exp2(score * score_factor), 0.0) for score in scores]
        values = [
            jnp.dot(
                weight.astype(jnp.bfloat16), kv[1, pl.ds(base, GROUP), span_of],
                preferred_element_type=jnp.float32,
            )
            for weight, span_of in zip(weights, spans)
        ]
        for weight, value, span_of in zip(weights, values, spans):
            den[pl.ds(base, GROUP), span_of] = weight
            num[pl.ds(base, GROUP), span_of] = value
        return carry

    def memory_group(g):
        base = g * GROUP
        window = 2 * g
        start = phase * (rows // WIN)
        last = rows // WIN
        first_open = opened[0, start + window]
        second_open = opened[0, start + window + 1] if window + 1 <= last else first_open
        row = lax.broadcasted_iota(jnp.int32, (GROUP, MEM), 0)
        gate = jnp.where(row < WIN, first_open, second_open) == 1
        for i in range(heads):
            span_of = slice(i * HD, (i + 1) * HD)
            score = lax.dot_general(
                q[base:base + GROUP, span_of], mem[0, :, span_of],
                (((1,), (1,)), ((), ())), preferred_element_type=jnp.float32,
            )
            weight = jnp.where(gate, jnp.exp2(score * score_factor), 0.0)
            total = den[base:base + GROUP, span_of]
            for j in range(MEM // HD):
                total = total + weight[:, j * HD:(j + 1) * HD]
            denom = jnp.sum(total, axis=-1, keepdims=True)
            value = num[base:base + GROUP, span_of] + jnp.dot(
                weight.astype(jnp.bfloat16), mem[1, :, span_of],
                preferred_element_type=jnp.float32,
            )
            att[me, base:base + GROUP, span_of] = (value / denom).astype(jnp.bfloat16)

    def work():
        queries()
        frame_rows()
        halo.wait_recv()
        for g in range(groups):
            local_group(g, 0)

    @pl.when(c >= EARLY)
    def _():
        work()

    def relay_rows(first, last):
        for copy, relay in zip(wo_copies[first:last], wo_relays[first:last]):
            copy.wait_recv()
            relay.start()

    early_relays = len(wo_relays) // 2
    relay_rows(0, early_relays)
    for k in range(PIECES):
        chain_piece(k)
    relay_rows(early_relays, len(wo_relays))

    @pl.when(c < EARLY)
    def _():
        work()

    for k in range(PIECES):
        moved[k].wait_recv()

    bounds = [HALF] + [GROUP * g for g in range(1, groups - 1)] + [HALF + rows]
    members = [[g] for g in range(groups - 2)] + [[groups - 2, groups - 1]]
    sides, crosses, relays = [], [], []
    for j, inside in enumerate(members):
        at = pl.ds(bounds[j], bounds[j + 1] - bounds[j])
        for g in inside:
            memory_group(g)
        copy = remote(att.at[me, at], att.at[me, at], a_send.at[j], a_recv.at[j], {"mp": sib})
        copy.start()
        sides.append(copy)
        across, passed = [], []
        for o in range(1, chips):
            to = (me + 2 * o) % n_mp
            source = (me + n_mp - 2 * o) % n_mp
            copy = remote(att.at[me, at], att.at[me, at], c_send.at[j, o - 1], c_recv.at[j, o - 1], {"mp": to})
            copy.start()
            across.append(copy)
            passed.append(remote(
                att.at[source, at], att.at[source, at], r_send.at[j, o - 1], r_recv.at[j, o - 1], {"mp": sib},
            ))
        crosses.append(across)
        relays.append(passed)

    wo_own.wait()
    for copy in wo_relays + wo_middles + [wo_side]:
        copy.wait_recv()

    def finish(j):
        sides[j].wait_recv()
        for copy in relays[j]:
            copy.wait_recv()
        first, count = bounds[j], bounds[j + 1] - bounds[j]
        own = pl.ds(pl.multiple_of(me * share, HD), share)
        total = x[first - HALF:first - HALF + count, own].astype(jnp.float32)
        for m in range(n_mp):
            total = total + jnp.dot(
                att[m, first:first + count, :], wo[m], preferred_element_type=jnp.float32
            )
        out[first - HALF:first - HALF + count, :] = total.astype(jnp.bfloat16)

    for j in range(len(members)):
        for o in range(chips - 1):
            crosses[j][o].wait_recv()
            relays[j][o].start()
        if j > 0:
            finish(j - 1)
    finish(len(members) - 1)

    for copy in wo_copies + wo_middles + wo_relays + tails + moved + sides + [halo, wo_side]:
        copy.wait_send()
    for group in crosses + relays:
        for copy in group:
            copy.wait_send()

    @pl.when(c < n_span - 1)
    def _():
        for copy in chain:
            copy.wait_send()


def local(n_span, n_mp, latents, w_qkv, w_out, decay, frame_ids, memory_mask):
    rows, width = latents.shape
    cols = w_qkv.shape[2]
    share = width // n_mp
    ext = -(-(rows + WIN) // GROUP) * GROUP
    groups = ext // GROUP
    count = groups - 1
    others = max(n_mp // 2 - 1, 1)
    any_spec = pl.BlockSpec(memory_space=pltpu.HBM)
    vmem_spec = pl.BlockSpec(memory_space=pltpu.VMEM)
    dma = pltpu.SemaphoreType.DMA
    flops = 2 * rows * width * 4 * cols
    return pl.pallas_call(
        functools.partial(body, (n_span, n_mp, rows, width, cols)),
        out_shape=jax.ShapeDtypeStruct((rows, share), jnp.bfloat16),
        in_specs=[any_spec] * 6,
        out_specs=vmem_spec,
        scratch_shapes=[
            pltpu.VMEM(decay.shape[1:], jnp.float32),
            pltpu.VMEM(frame_ids.shape, jnp.int32),
            pltpu.SMEM(memory_mask.shape, jnp.int32),
            pltpu.VMEM((rows, width), jnp.bfloat16),
            pltpu.VMEM((width, 3 * cols), jnp.bfloat16),
            pltpu.VMEM((n_mp, cols, share), jnp.bfloat16),
            pltpu.VMEM((2, ext, cols), jnp.bfloat16),
            pltpu.VMEM((ext, cols), jnp.bfloat16),
            pltpu.VMEM((ext, cols), jnp.float32),
            pltpu.VMEM((ext, cols), jnp.float32),
            pltpu.VMEM((n_mp, ext, cols), jnp.bfloat16),
            pltpu.VMEM((groups, 8, GROUP), jnp.float32),
            pltpu.VMEM((MEM, cols), jnp.bfloat16),
            pltpu.VMEM((MEM, cols), jnp.bfloat16),
            pltpu.VMEM((MEM, cols), jnp.bfloat16),
            pltpu.VMEM((MEM, cols), jnp.bfloat16),
            pltpu.VMEM((2, MEM, cols), jnp.bfloat16),
            dma((9,)),
            dma, dma,
            dma((2 * others,)), dma((2 * others,)),
            dma((2 * others,)), dma((2 * others,)),
            dma((2 * others,)), dma((2 * others,)),
            dma((PIECES,)), dma((PIECES,)),
            dma((PIECES,)), dma((PIECES,)),
            dma((PIECES,)), dma((PIECES,)),
            dma, dma,
            dma((count,)), dma((count,)),
            dma((count, others)), dma((count, others)),
            dma((count, others)), dma((count, others)),
        ],
        compiler_params=pltpu.CompilerParams(
            collective_id=0, has_side_effects=True, vmem_limit_bytes=40 * 1024 * 1024
        ),
        cost_estimate=pl.CostEstimate(flops=flops, bytes_accessed=12 << 20, transcendentals=1 << 20),
        name="refiner",
    )(
        *[pltpu.with_memory_space_constraint(a, pltpu.HBM) for a in (latents, jnp.transpose(w_qkv, (1, 0, 2)), w_out,
        decay.reshape(decay.shape[1:]), frame_ids, memory_mask)]
    )


def solution(mesh):
    return jax.shard_map(
        functools.partial(local, mesh.shape["span"], mesh.shape["mp"]),
        mesh=mesh,
        in_specs=(
            P(("span", "phase"), None),
            P(None, None, "mp"),
            P("mp", None),
            P("span", None, "mp"),
            P("span", None),
            P("span", None),
        ),
        out_specs=P(("span", "phase"), "mp"),
        check_vma=False,
    )
```

```python
import contextlib
import functools
import math

import jax
import jax.numpy as jnp
from jax import lax
from jax.experimental import pallas as pl
from jax.experimental.pallas import tpu as pltpu
from jax.sharding import PartitionSpec as P

HD = 128
WIN = 64
MEM = 256
HALF = WIN // 2
GROUP = 128
CUTS = 4
KPARTS = 4
PLAN = ((0, 1, 2), (1, 2, 3), (2, 3, 5), (3, 4, 6))
MESH = pl.DeviceIdType.MESH

outside_frame = 1048576
epsilon = 1e-06
score_factor = HD ** (-0.5) * math.log2(math.e)


@contextlib.contextmanager
def scope(name):
    yield


def remote(src, dst, send, recv, where):
    return pltpu.make_async_remote_copy(
        src_ref=src, dst_ref=dst, send_sem=send, recv_sem=recv,
        device_id=where, device_id_type=MESH,
    )


def body(
    sizes, x_hbm, w_hbm, wo_hbm, decay_hbm, frames_hbm, opened_hbm, out,
    decay, frames, opened, x, w, wo, kv, q, num, den, att, acc, fr, tail_in, s_in, s_out, m_out, mem,
    load_sem, ws_send, ws_recv, wo_send, wo_recv, wd_send, wu_send, wr_recv, y_send, y_recv, z_send, z_recv, m_send, m_recv,
    h_send, h_recv, a_send, a_recv, c_send, c_recv, r_send, r_recv,
):
    n_span, n_mp, rows, width, cols = sizes
    heads = cols // HD
    share = width // n_mp
    groups = kv.shape[2] // GROUP
    c = lax.axis_index("span")
    me = lax.axis_index("mp")
    phase = lax.axis_index("phase")
    is0 = phase == 0
    other = 1 - phase
    kept, sent = phase, 1 - phase
    sib = me + 1 - 2 * (me % 2)
    chips = n_mp // 2
    top = rows - MEM
    tail0 = HALF + top
    piece = MEM // CUTS
    last = n_span - 1

    barrier = pltpu.get_barrier_semaphore()
    for o in range(1, n_mp):
        pl.semaphore_signal(barrier, inc=1, device_id={"mp": (me + o) % n_mp}, device_id_type=MESH)
    pl.semaphore_signal(barrier, inc=1, device_id={"phase": other}, device_id_type=MESH)

    @pl.when(c > 0)
    def _():
        pl.semaphore_signal(barrier, inc=1, device_id={"span": c - 1}, device_id_type=MESH)

    @pl.when(c < last)
    def _():
        pl.semaphore_signal(barrier, inc=1, device_id={"span": c + 1}, device_id_type=MESH)

    def load(i, src, dst):
        copy = pltpu.make_async_copy(src, dst, load_sem.at[i])
        copy.start()
        return copy

    deep = width // KPARTS
    for n in range(KPARTS):
        at = pl.ds(n * deep, deep)
        load(n, x_hbm.at[pl.ds(top, MEM), at], x.at[pl.ds(top, MEM), at])
        load(n, w_hbm.at[1 + sent, at], w.at[at, pl.ds(0, cols)])
    late = KPARTS
    both_parts = w.at[pl.ds(0, deep), pl.ds(0, MEM + cols)]

    zero_rows = kv.shape[2] - (HALF + rows + HALF)
    kv[:, :, HALF + rows + HALF:, :] = jnp.zeros((2, heads, zero_rows, HD), jnp.bfloat16)
    q[:, HALF + rows:, :] = jnp.zeros((heads, q.shape[1] - HALF - rows, HD), jnp.bfloat16)
    q[:, :HALF, :] = jnp.zeros((heads, HALF, HD), jnp.bfloat16)
    blank = pl.multiple_of(phase * (HALF + rows), HALF)
    kv[:, :, pl.ds(blank, HALF), :] = jnp.zeros((2, heads, HALF, HD), jnp.bfloat16)

    @pl.when(c == 0)
    def _():
        s_in[...] = jnp.zeros(s_in.shape, s_in.dtype)

    block = HD // 2
    parity = (c + phase) % 2

    def columns_of(m):
        return pl.ds(pl.multiple_of(m * share, HD), share)

    wo_copies, wo_downs, wo_ups, wo_acrosses, far = [], [], [], [], []
    for o in range(1, chips):
        for near in (me, sib):
            far.append((near + n_mp - 2 * o) % n_mp)
    for i in range(heads):
        part = pl.ds(pl.multiple_of(i * HD + parity * block, block), block)
        for o in range(1, chips):
            for near in (me, sib):
                to, source = (near + 2 * o) % n_mp, (near + n_mp - 2 * o) % n_mp
                at = len(wo_copies)
                wo_copies.append(remote(
                    wo_hbm.at[part, columns_of(to)], wo.at[me, part],
                    wo_send, wo_recv.at[at], {"mp": to},
                ))
                held = wo.at[source, part]
                wo_downs.append(remote(held, held, wd_send, wr_recv.at[i], {"span": (c + last) % n_span}))
                if i == 0:
                    wo_acrosses.append(remote(held, held, wu_send, wr_recv.at[i], {"phase": other}))
                else:
                    wo_ups.append(remote(held, held, wu_send, wr_recv.at[i], {"span": (c + 1) % n_span}))
    wo_side = remote(wo_hbm.at[:, columns_of(sib)], wo.at[me], ws_send, ws_recv, {"mp": sib})
    per_head = len(far)

    def relay(at):
        with scope("relay"):
            wo_copies[at].wait_recv()

        @pl.when(c > 0)
        def _():
            wo_downs[at].start()

        if at < per_head:
            @pl.when(c == last)
            def _():
                wo_acrosses[at].start()

    def relay_up(first, end):
        @pl.when(c == last - 1)
        def _():
            for at in range(first, end):
                wo_ups[at - per_head].start()

    def unit(part, flag):
        scale = lax.rsqrt(jnp.mean(part * part, axis=-1, keepdims=True) + epsilon)
        if flag is not None:
            scale = jnp.where(flag, scale, 1.0)
        return (part * scale).astype(jnp.bfloat16)

    def project(first, count, column, size):
        return jnp.dot(
            x[first:first + count, :], w[:, column:column + size],
            preferred_element_type=jnp.float32,
        )

    def tail_copy(k, i, r):
        return remote(
            kv.at[sent, i, pl.ds(tail0 + r * piece, piece)], tail_in.at[i, pl.ds(r * piece, piece)],
            y_send, y_recv.at[k], {"phase": other},
        )

    def chain_copy(k, i, r):
        at = pl.ds(r * piece, piece)
        return remote(s_out.at[i, at], s_in.at[i, at], z_send, z_recv.at[k], {"span": (c + 1) % n_span})

    def moved_copy(k, i, r):
        at = pl.ds(r * piece, piece)
        return remote(m_out.at[i, at], mem.at[kept, i, at], m_send, m_recv.at[i], {"phase": other})

    def each(make):
        return [make(i * CUTS + r, i, r) for i in range(heads) for r in range(CUTS)]

    tails = each(tail_copy)

    def keep(raw, first, count, n, at):
        which = sent if n < heads else kept
        part = raw[:, at * HD:(at + 1) * HD]
        kv[which, n % heads, HALF + first:HALF + first + count, :] = unit(part, which == 0)

    def send_tail(i):
        for r in range(CUTS):
            tails[i * CUTS + r].start()

    raw = None
    for n in range(KPARTS):
        with scope("load%d" % n):
            pltpu.make_async_copy(both_parts, both_parts, load_sem.at[n]).wait()
        if n == 0:
            w_kept = load(late, w_hbm.at[1 + kept], w.at[:, pl.ds(cols, cols)])
        if n == 1:
            small = [
                load(late + 1, decay_hbm, decay), load(late + 2, frames_hbm, frames),
                load(late + 3, opened_hbm, opened),
            ]
            x_head = load(late + 4, x_hbm.at[pl.ds(0, top)], x.at[pl.ds(0, top)])
        if n == KPARTS - 1:
            with scope("bar"):
                pl.semaphore_wait(barrier, n_mp + 1 + (c + n_span - 1) // n_span - (c + 1) // n_span)
            for copy in wo_copies:
                copy.start()
        at = slice(n * deep, (n + 1) * deep)
        with scope("sent%d" % n):
            step = jnp.dot(x[top:, at], w[at, :HD], preferred_element_type=jnp.float32)
            raw = step if raw is None else raw + step
    with scope("unit"):
        keep(raw, top, MEM, 0, 0)
    send_tail(0)
    wo_side.start()
    w_query = load(late + 5, w_hbm.at[0], w.at[:, pl.ds(2 * cols, cols)])
    wo_own = load(late + 6, wo_hbm.at[:, columns_of(me)], wo.at[me])
    with scope("sentrest"):
        raw = project(top, MEM, HD, cols - HD)
        for i in range(1, heads):
            keep(raw, top, MEM, i, i - 1)
    with scope("loadk"):
        w_kept.wait()
    with scope("kept"):
        raw = project(top, MEM, cols, cols)
        for i in range(heads):
            keep(raw, top, MEM, heads + i, i)
    with scope("loadh"):
        x_head.wait()

    def head_rows(pair):
        with scope("headkv"):
            raw = project(0, top, pair * HD, 2 * HD)
            for at in range(2):
                keep(raw, 0, top, pair + at, at)

    for copy in small:
        copy.wait()
    halo_from = pl.multiple_of(HALF + other * (rows - HALF), HALF)
    halo = remote(
        kv.at[:, :, pl.ds(halo_from, HALF)], kv.at[:, :, pl.ds(blank, HALF)],
        h_send, h_recv, {"phase": other},
    )

    def rate_of(half, i):
        rate = decay[half:half + 1, 0:1]
        for n in range(1, heads):
            rate = jnp.where(i == n, decay[half:half + 1, n:n + 1], rate)
        return jnp.broadcast_to(rate, (1, HD))

    def mix(rate):
        return jnp.where(is0, 1.0 - rate, jnp.sqrt(1.0 - rate * rate))

    def chain_head(i):
        r0, r1 = rate_of(0, i), rate_of(1, i)
        f0, f1, both = mix(r0), mix(r1), r0 * r1
        for r in range(CUTS):
            k = i * CUTS + r
            rows_at = pl.ds(r * piece, piece)
            own = kv[kept, i, tail0 + r * piece:tail0 + (r + 1) * piece, :].astype(jnp.float32)
            with scope("waittail"):
                tail_copy(k, i, r).wait_recv()
            theirs = tail_in[i, rows_at, :].astype(jnp.float32)
            low = f0 * jnp.where(is0, own, theirs)
            high = r1 * low + f1 * jnp.where(is0, theirs, own)

            @pl.when(c > 0)
            def _():
                with scope("waitchain"):
                    chain_copy(k, i, r).wait_recv()

            state = s_in[i, rows_at, :].astype(jnp.float32)
            s_out[i, rows_at, :] = (both * state + high).astype(jnp.bfloat16)

            @pl.when(c < last)
            def _():
                chain_copy(k, i, r).start()

            later = r0 * state + low
            m_out[i, rows_at, :] = jnp.where(is0, later, state).astype(jnp.bfloat16)
            moved_copy(k, i, r).start()
            mem[kept, i, rows_at, :] = jnp.where(is0, state, later).astype(jnp.bfloat16)

    def queries(first, count):
        with scope("queries"):
            raw = project(first, count, 2 * cols, cols)
            for i in range(heads):
                q[i, HALF + first:HALF + first + count, :] = unit(raw[:, i * HD:(i + 1) * HD], None)

    def frame_rows():
        total = frames.shape[1]
        wide = jnp.broadcast_to(frames[...], (8, total))
        ahead = pltpu.roll(wide, HALF, 1)
        behind = pltpu.roll(wide, total - (rows - HALF), 1)
        place = lax.broadcasted_iota(jnp.int32, wide.shape, 1)
        ext = jnp.where(is0, ahead, behind)
        least = jnp.where(is0, HALF, 0)
        limit = jnp.where(is0, total + HALF, rows + HALF)
        ext = jnp.where((place >= least) & (place < limit), ext, outside_frame)
        for g in range(groups):
            fr[g] = ext[:, g * GROUP:(g + 1) * GROUP].astype(jnp.float32)

    def local_group(g):
        at = pl.ds(g * GROUP, GROUP)
        key_frame = jnp.broadcast_to(fr[g][0:1, :], (GROUP, GROUP))
        same = (
            lax.broadcasted_iota(jnp.int32, (GROUP, GROUP), 0) // WIN
            == lax.broadcasted_iota(jnp.int32, (GROUP, GROUP), 1) // WIN
        )
        allowed = same & (key_frame <= key_frame.T)
        scores = [
            lax.dot_general(
                q[i, at, :], kv[0, i, at, :],
                (((1,), (1,)), ((), ())), preferred_element_type=jnp.float32,
            )
            for i in range(heads)
        ]
        weights = [jnp.where(allowed, jnp.exp2(score * score_factor), 0.0) for score in scores]
        values = [
            jnp.dot(weights[i].astype(jnp.bfloat16), kv[1, i, at, :], preferred_element_type=jnp.float32)
            for i in range(heads)
        ]
        for i in range(heads):
            den[i, at, :] = weights[i]
            num[i, at, :] = values[i]

    spots = [(i, n * 2 * GROUP, 2 * GROUP) for i in range(heads - 1) for n in range(rows // (2 * GROUP))]
    spots += [(heads - 1, n * GROUP, GROUP) for n in range(rows // GROUP)]
    sides, crosses, relays = [], [], []
    for j, (i, first, count) in enumerate(spots):
        at = pl.ds(first, count)
        mine = att.at[me, i, at]
        sides.append(remote(mine, mine, a_send, a_recv, {"mp": sib}))
        across, passed = [], []
        for o in range(1, chips):
            to = (me + 2 * o) % n_mp
            theirs = att.at[(me + n_mp - 2 * o) % n_mp, i, at]
            across.append(remote(mine, mine, c_send, c_recv.at[j, o - 1], {"mp": to}))
            passed.append(remote(theirs, theirs, r_send, r_recv.at[max(j - len(spots) + rows // GROUP + 1, 0)], {"mp": sib}))
        crosses.append(across)
        relays.append(passed)

    start = phase * (rows // WIN)

    def memory_groups(i, members):
        scores, flagged = [], []
        for g in members:
            window = start + g * (GROUP // WIN)
            row = lax.broadcasted_iota(jnp.int32, (GROUP, MEM), 0)
            flags = opened[0, window + GROUP // WIN]
            for n in range(GROUP // WIN - 1, -1, -1):
                flags = jnp.where(row < HALF + n * WIN, opened[0, window + n], flags)
            flagged.append(flags == 1)
            scores.append(lax.dot_general(
                q[i, HALF + g * GROUP:HALF + (g + 1) * GROUP, :], mem[0, i],
                (((1,), (1,)), ((), ())), preferred_element_type=jnp.float32,
            ))
        weights = [
            jnp.where(flags, jnp.exp2(score * score_factor), 0.0) for score, flags in zip(scores, flagged)
        ]
        values = [
            jnp.dot(weight.astype(jnp.bfloat16), mem[1, i], preferred_element_type=jnp.float32)
            for weight in weights
        ]
        for g, weight, value in zip(members, weights, values):
            at = slice(HALF + g * GROUP, HALF + (g + 1) * GROUP)
            total = den[i, at, :]
            for j in range(MEM // HD):
                total = total + weight[:, j * HD:(j + 1) * HD]
            denom = jnp.sum(total, axis=-1, keepdims=True)
            att[me, i, g * GROUP:(g + 1) * GROUP, :] = ((num[i, at, :] + value) / denom).astype(jnp.bfloat16)

    def memory_head(i):
        with scope("waitmem"):
            remote(m_out.at[i], mem.at[kept, i], m_send, m_recv.at[i], {"phase": other}).wait_recv()
        with scope("mem"):
            for base in range(0, rows, 2 * GROUP):
                memory_groups(i, [base // GROUP, base // GROUP + 1])
                for j, (which, first, count) in enumerate(spots):
                    if which == i and base <= first < base + 2 * GROUP:
                        for copy in crosses[j]:
                            copy.start()
                        sides[j].start()

    def relay_head(i, n):
        for at in range(i * per_head + n * per_head // 2, i * per_head + (n + 1) * per_head // 2):
            relay(at)

    end = heads * per_head
    plan = {}
    for kind, spots_of in enumerate(PLAN):
        for i, place in enumerate(spots_of):
            plan.setdefault(place, []).append((kind, i))

    def chain_at(place):
        kind, i = jnp.minimum(c, len(PLAN) - 1), jnp.int32(heads)
        for which, head in plan[place]:
            if head < heads:
                i = jnp.where(kind == which, head, i)

        @pl.when(i < heads)
        def _():
            with scope("chain%d" % place):
                chain_head(i)

    for pair in range(0, 2 * heads, 2):
        head_rows(pair)
        if pair == 0:
            send_tail(1)
    halo.start()
    chain_at(0)
    with scope("loadq"):
        w_query.wait()
    queries(0, top)
    for i in range(2, heads):
        send_tail(i)
    relay_head(0, 0)
    queries(top, rows - top)
    chain_at(1)
    relay_head(0, 1)
    with scope("local"):
        frame_rows()
        for g in range(1, groups - 1):
            local_group(g)
        with scope("halo"):
            halo.wait_recv()
        local_group(0)
        local_group(groups - 1)
    chain_at(2)
    relay_head(1, 0)
    chain_at(3)
    relay_head(1, 1)
    chain_at(4)
    relay_head(2, 0)
    memory_head(0)
    chain_at(5)
    relay_up(per_head, 2 * per_head + per_head // 2)
    chain_at(6)
    relay_head(2, 1)
    memory_head(1)
    relay_up(2 * per_head + per_head // 2, heads * per_head)
    memory_head(2)

    own = pl.ds(pl.multiple_of(me * share, HD), share)

    def product(sources, which, first, count):
        left = jnp.concatenate([att[m, i, first:first + count, :] for m in sources for i in which], axis=1)
        right = jnp.concatenate([wo[m, i * HD:(i + 1) * HD, :] for m in sources for i in which], axis=0)
        return jnp.dot(left, right, preferred_element_type=jnp.float32)

    def add(sources, which, scope_name):
        with scope(scope_name):
            for first in range(0, rows, 2 * GROUP):
                at = slice(first, first + 2 * GROUP)
                acc[at, :] = acc[at, :] + product(sources, which, first, 2 * GROUP)

    def cross(j):
        for o in range(chips - 1):
            with scope("waitcross"):
                crosses[j][o].wait_recv()
            relays[j][o].start()

    def arrived(lot, which):
        with scope("waitrelay"):
            remote(lot, lot, r_send, r_recv.at[which], {"mp": sib}).wait_recv()

    def far_weights(i):
        with scope("waitwo"):
            lot = wo.at[pl.ds(0, chips - 1), pl.ds(0, HD)]
            remote(lot, lot, wd_send, wr_recv.at[i], {"phase": other}).wait_recv()

    order = [[j for j, spot in enumerate(spots) if spot[0] == i] for i in range(heads)]
    wo_own.wait()
    with scope("own"):
        for first in range(0, rows, 2 * GROUP):
            at = slice(first, first + 2 * GROUP)
            acc[at, :] = x[at, own].astype(jnp.float32) + product([me], range(heads), first, 2 * GROUP)
    early = range(heads - 1)
    for i in early:
        for j in order[i]:
            cross(j)
    with scope("waitside"):
        wo_side.wait_recv()
        remote(att.at[me], att.at[me], a_send, a_recv, {"mp": sib}).wait_recv()
    add([sib], range(heads), "near")
    for i in early:
        far_weights(i)
    add(far[0::2], early, "direct")
    final = order[heads - 1]
    for j in final[:2]:
        cross(j)
    arrived(att.at[pl.ds(0, chips - 1), pl.ds(0, heads - 1)], 0)
    add(far[1::2], early, "passed")
    far_weights(heads - 1)
    for n, j in enumerate(final):
        if n + 2 < len(final):
            cross(final[n + 2])
        first, count = spots[j][1], spots[j][2]
        arrived(att.at[pl.ds(0, chips - 1), heads - 1, pl.ds(first, count)], 1 + n)
        with scope("fin"):
            at = slice(first, first + count)
            out[at, :] = (acc[at, :] + product(far, [heads - 1], first, count)).astype(jnp.bfloat16)

    with scope("sends"):
        tail_all = kv.at[sent, :, pl.ds(tail0, MEM)]
        wo_all = wo.at[pl.ds(0, chips - 1)]
        att_all = att.at[pl.ds(0, chips - 1)]
        for src, send, recv, where in (
            (tail_all, y_send, y_recv.at[0], {"phase": other}),
            (m_out, m_send, m_recv.at[0], {"phase": other}),
            (wo_all, wo_send, wo_recv.at[0], {"mp": sib}),
            (att.at[me], a_send, a_recv, {"mp": sib}),
            (att_all, c_send, c_recv.at[0, 0], {"mp": sib}),
            (att_all, r_send, r_recv.at[0], {"mp": sib}),
        ):
            remote(src, src, send, recv, where).wait_send()
        halo.wait_send()
        wo_side.wait_send()

        @pl.when(c < last)
        def _():
            remote(s_out, s_in, z_send, z_recv.at[0], {"phase": other}).wait_send()

        @pl.when(c > 0)
        def _():
            remote(wo_all, wo_all, wd_send, wr_recv.at[0], {"phase": other}).wait_send()

        @pl.when(c == last - 1)
        def _():
            lot = wo.at[pl.ds(0, chips - 1), pl.ds(0, (heads - 1) * HD)]
            remote(lot, lot, wu_send, wr_recv.at[0], {"phase": other}).wait_send()

        @pl.when(c == last)
        def _():
            lot = wo.at[pl.ds(0, chips - 1), pl.ds(0, HD)]
            remote(lot, lot, wu_send, wr_recv.at[0], {"phase": other}).wait_send()


def local(n_span, n_mp, latents, w_qkv, w_out, decay, frame_ids, memory_mask):
    rows, width = latents.shape
    cols = w_qkv.shape[2]
    heads = cols // HD
    share = width // n_mp
    ext = -(-(rows + WIN) // GROUP) * GROUP
    groups = ext // GROUP
    others = max(n_mp // 2 - 1, 1)
    chunks = 2 * others * heads
    pieces = heads * CUTS
    spots = (heads - 1) * (rows // (2 * GROUP)) + rows // GROUP
    hbm_spec = pl.BlockSpec(memory_space=pltpu.HBM)
    dma = pltpu.SemaphoreType.DMA
    bf16, f32 = jnp.bfloat16, jnp.float32
    flops = 2 * rows * width * 4 * cols
    inputs = (
        latents, jnp.transpose(w_qkv, (1, 0, 2)), w_out,
        decay.reshape(decay.shape[1:]), frame_ids, memory_mask,
    )
    return pl.pallas_call(
        functools.partial(body, (n_span, n_mp, rows, width, cols)),
        out_shape=jax.ShapeDtypeStruct((rows, share), bf16),
        in_specs=[hbm_spec] * 6,
        out_specs=pl.BlockSpec(memory_space=pltpu.VMEM),
        scratch_shapes=[
            pltpu.VMEM(decay.shape[1:], f32),
            pltpu.VMEM(frame_ids.shape, jnp.int32),
            pltpu.SMEM(memory_mask.shape, jnp.int32),
            pltpu.VMEM((rows, width), bf16),
            pltpu.VMEM((width, 3 * cols), bf16),
            pltpu.VMEM((n_mp, cols, share), bf16),
            pltpu.VMEM((2, heads, ext, HD), bf16),
            pltpu.VMEM((heads, ext, HD), bf16),
            pltpu.VMEM((heads, ext, HD), f32),
            pltpu.VMEM((heads, ext, HD), f32),
            pltpu.VMEM((n_mp, heads, rows, HD), bf16),
            pltpu.VMEM((rows, share), f32),
            pltpu.VMEM((groups, 8, GROUP), f32),
            pltpu.VMEM((heads, MEM, HD), bf16),
            pltpu.VMEM((heads, MEM, HD), bf16),
            pltpu.VMEM((heads, MEM, HD), bf16),
            pltpu.VMEM((heads, MEM, HD), bf16),
            pltpu.VMEM((2, heads, MEM, HD), bf16),
            dma((KPARTS + 7,)),
            dma, dma,
            dma, dma((chunks,)), dma, dma, dma((heads,)),
            dma, dma((pieces,)),
            dma, dma((pieces,)),
            dma, dma((heads,)),
            dma, dma,
            dma, dma,
            dma, dma((spots, others)),
            dma, dma((1 + rows // GROUP,)),
        ],
        compiler_params=pltpu.CompilerParams(
            collective_id=0, has_side_effects=True, vmem_limit_bytes=40 * 1024 * 1024
        ),
        cost_estimate=pl.CostEstimate(flops=flops, bytes_accessed=12 << 20, transcendentals=1 << 20),
        name="refiner",
    )(*[pltpu.with_memory_space_constraint(a, pltpu.HBM) for a in inputs])


def solution(mesh):
    return jax.shard_map(
        functools.partial(local, mesh.shape["span"], mesh.shape["mp"]),
        mesh=mesh,
        in_specs=(
            P(("span", "phase"), None),
            P(None, None, "mp"),
            P("mp", None),
            P("span", None, "mp"),
            P("span", None),
            P("span", None),
        ),
        out_specs=P(("span", "phase"), "mp"),
        check_vma=False,
    )
```

```python
import contextlib
import functools
import math

import jax
import jax.numpy as jnp
from jax import lax
from jax.experimental import pallas as pl
from jax.experimental.pallas import tpu as pltpu
from jax.sharding import PartitionSpec as P

HD = 128
WIN = 64
MEM = 256
HALF = WIN // 2
GROUP = 128
CUTS = 4
KPARTS = 2
PLAN = ((0, 1, 3), (2, 4, 5), (4, 5, 6), (5, 6, 7))
MESH = pl.DeviceIdType.MESH

outside_frame = 1048576
epsilon = 1e-06
score_factor = HD ** (-0.5) * math.log2(math.e)


@contextlib.contextmanager
def scope(name):
    yield


def remote(src, dst, send, recv, where):
    return pltpu.make_async_remote_copy(
        src_ref=src, dst_ref=dst, send_sem=send, recv_sem=recv,
        device_id=where, device_id_type=MESH,
    )


def body(
    sizes, x_hbm, w_hbm, wo_hbm, decay_hbm, frames_hbm, opened_hbm, out,
    decay, frames, opened, x, w, wo, kv, q, num, den, att, acc, fr, tail_in, s_in, s_out, m_out, mem,
    load_sem, ws_send, ws_recv, wo_send, wo_recv, wd_send, wu_send, wr_recv, y_send, y_recv, z_send, z_recv, m_send, m_recv,
    h_send, h_recv, a_send, a_recv, c_send, c_recv, r_send, r_recv,
):
    n_span, n_mp, rows, width, cols = sizes
    heads = cols // HD
    share = width // n_mp
    groups = kv.shape[2] // GROUP
    c = lax.axis_index("span")
    me = lax.axis_index("mp")
    phase = lax.axis_index("phase")
    is0 = phase == 0
    other = 1 - phase
    kept, sent = phase, 1 - phase
    sib = me + 1 - 2 * (me % 2)
    chips = n_mp // 2
    top = rows - MEM
    tail0 = HALF + top
    piece = MEM // CUTS
    last = n_span - 1

    barrier = pltpu.get_barrier_semaphore()
    for o in range(1, n_mp):
        pl.semaphore_signal(barrier, inc=1, device_id={"mp": (me + o) % n_mp}, device_id_type=MESH)
    pl.semaphore_signal(barrier, inc=1, device_id={"phase": other}, device_id_type=MESH)

    @pl.when(c > 0)
    def _():
        pl.semaphore_signal(barrier, inc=1, device_id={"span": c - 1}, device_id_type=MESH)

    @pl.when(c < last)
    def _():
        pl.semaphore_signal(barrier, inc=1, device_id={"span": c + 1}, device_id_type=MESH)

    def load(i, src, dst):
        copy = pltpu.make_async_copy(src, dst, load_sem.at[i])
        copy.start()
        return copy

    deep = width // KPARTS
    for n in range(KPARTS):
        at = pl.ds(n * deep, deep)
        load(n, x_hbm.at[pl.ds(top, MEM), at], x.at[pl.ds(top, MEM), at])
        load(n, w_hbm.at[1 + sent, at, pl.ds(0, HD)], w.at[at, pl.ds(0, HD)])
    both_parts = w.at[pl.ds(0, deep), pl.ds(0, MEM + HD)]
    w_sent = load(KPARTS, w_hbm.at[1 + sent, :, pl.ds(HD, cols - HD)], w.at[:, pl.ds(HD, cols - HD)])
    w_kept = load(KPARTS + 1, w_hbm.at[1 + kept], w.at[:, pl.ds(cols, cols)])
    w_query = load(KPARTS + 2, w_hbm.at[0], w.at[:, pl.ds(2 * cols, cols)])
    small = [
        load(KPARTS + 3, decay_hbm, decay), load(KPARTS + 4, frames_hbm, frames), load(KPARTS + 5, opened_hbm, opened),
    ]
    x_head = load(KPARTS + 6, x_hbm.at[pl.ds(0, top)], x.at[pl.ds(0, top)])
    wo_own = load(KPARTS + 7, wo_hbm.at[:, pl.ds(pl.multiple_of(me * share, HD), share)], wo.at[me])

    zero_rows = kv.shape[2] - (HALF + rows + HALF)
    kv[:, :, HALF + rows + HALF:, :] = jnp.zeros((2, heads, zero_rows, HD), jnp.bfloat16)
    q[:, HALF + rows:, :] = jnp.zeros((heads, q.shape[1] - HALF - rows, HD), jnp.bfloat16)
    q[:, :HALF, :] = jnp.zeros((heads, HALF, HD), jnp.bfloat16)
    blank = pl.multiple_of(phase * (HALF + rows), HALF)
    kv[:, :, pl.ds(blank, HALF), :] = jnp.zeros((2, heads, HALF, HD), jnp.bfloat16)

    @pl.when(c == 0)
    def _():
        s_in[...] = jnp.zeros(s_in.shape, s_in.dtype)

    block = HD // 2
    parity = (c + phase) % 2

    def columns_of(m):
        return pl.ds(pl.multiple_of(m * share, HD), share)

    wo_copies, wo_downs, wo_ups, wo_acrosses, far = [], [], {}, [], []
    acrosses = range(chips - 1, 2 * (chips - 1))
    for o in range(1, chips):
        for near in (me, sib):
            far.append((near + n_mp - 2 * o) % n_mp)
    for i in range(heads):
        part = pl.ds(pl.multiple_of(i * HD + parity * block, block), block)
        for o in range(1, chips):
            for near in (me, sib):
                to, source = (near + 2 * o) % n_mp, (near + n_mp - 2 * o) % n_mp
                at = len(wo_copies)
                wo_copies.append(remote(
                    wo_hbm.at[part, columns_of(to)], wo.at[me, part],
                    wo_send, wo_recv.at[at], {"mp": to},
                ))
                held = wo.at[source, part]
                wo_downs.append(remote(held, held, wd_send, wr_recv.at[i], {"span": (c + last) % n_span}))
                if at in acrosses:
                    wo_acrosses.append(remote(held, held, wu_send, wr_recv.at[i], {"phase": other}))
                else:
                    wo_ups[at] = remote(held, held, wu_send, wr_recv.at[i], {"span": (c + 1) % n_span})
    wo_side = remote(wo_hbm.at[:, columns_of(sib)], wo.at[me], ws_send, ws_recv, {"mp": sib})
    per_head = len(far)

    def relay(at):
        with scope("relay"):
            wo_copies[at].wait_recv()

        @pl.when(c > 0)
        def _():
            wo_downs[at].start()

        if at in acrosses:
            @pl.when(c == last)
            def _():
                wo_acrosses[at - acrosses[0]].start()

    def relay_up(first, end):
        @pl.when(c == last - 1)
        def _():
            for at in range(first, end):
                wo_ups[at].start()

    def unit(part, flag):
        scale = lax.rsqrt(jnp.mean(part * part, axis=-1, keepdims=True) + epsilon)
        if flag is not None:
            scale = jnp.where(flag, scale, 1.0)
        return (part * scale).astype(jnp.bfloat16)

    def project(first, count, column, size):
        return jnp.dot(
            x[first:first + count, :], w[:, column:column + size],
            preferred_element_type=jnp.float32,
        )

    def tail_copy(k, i, r):
        return remote(
            kv.at[sent, i, pl.ds(tail0 + r * piece, piece)], tail_in.at[i, pl.ds(r * piece, piece)],
            y_send, y_recv.at[k], {"phase": other},
        )

    def chain_copy(k, i, r):
        at = pl.ds(r * piece, piece)
        return remote(s_out.at[i, at], s_in.at[i, at], z_send, z_recv.at[k], {"span": (c + 1) % n_span})

    def moved_copy(k, i, r):
        at = pl.ds(r * piece, piece)
        return remote(m_out.at[i, at], mem.at[kept, i, at], m_send, m_recv.at[i], {"phase": other})

    def each(make):
        return [make(i * CUTS + r, i, r) for i in range(heads) for r in range(CUTS)]

    tails = each(tail_copy)

    def keep(raw, first, count, n, at):
        part = raw[:, at * HD:(at + 1) * HD]
        rows_at = slice(HALF + first, HALF + first + count)
        if n >= 2 * heads:
            q[n - 2 * heads, rows_at, :] = unit(part, None)
        else:
            which = sent if n < heads else kept
            kv[which, n % heads, rows_at, :] = unit(part, which == 0)

    def columns(first, count, n, end):
        raw = project(first, count, n * HD, (end - n) * HD)
        for at in range(end - n):
            keep(raw, first, count, n + at, at)

    def send_tail(i):
        for r in range(CUTS):
            tails[i * CUTS + r].start()

    begun = 0

    def send_columns(count):
        nonlocal begun
        for copy in wo_copies[begun:begun + count]:
            copy.start()
        begun += count

    raw = None
    for n in range(KPARTS):
        with scope("load%d" % n):
            pltpu.make_async_copy(both_parts, both_parts, load_sem.at[n]).wait()
        if n == KPARTS - 1:
            with scope("bar"):
                pl.semaphore_wait(barrier, n_mp + 1 + (c + n_span - 1) // n_span - (c + 1) // n_span)
            send_columns(2 * (chips - 1))
        with scope("sent%d" % n):
            for start in range(n * deep, (n + 1) * deep, deep // 2):
                at = slice(start, start + deep // 2)
                step = jnp.dot(x[top:, at], w[at, :HD], preferred_element_type=jnp.float32)
                raw = step if raw is None else raw + step
    with scope("unit"):
        keep(raw, top, MEM, 0, 0)
    send_tail(0)
    wo_side.start()
    for copy in small:
        copy.wait()
    wide = -(-(3 * heads - 1) // 2)
    with scope("loadk"):
        w_sent.wait()
        w_kept.wait()
    with scope("tail1"):
        columns(top, MEM, 1, 1 + wide)
    send_tail(1)
    send_columns(chips - 1)
    with scope("loadq"):
        w_query.wait()
    with scope("tail2"):
        columns(top, MEM, 1 + wide, 3 * heads)
    for i in range(2, heads):
        send_tail(i)
    with scope("loadx"):
        x_head.wait()
    halo_from = pl.multiple_of(HALF + other * (rows - HALF), HALF)
    halo = remote(
        kv.at[:, :, pl.ds(halo_from, HALF)], kv.at[:, :, pl.ds(blank, HALF)],
        h_send, h_recv, {"phase": other},
    )

    def rate_of(half, i):
        rate = decay[half:half + 1, 0:1]
        for n in range(1, heads):
            rate = jnp.where(i == n, decay[half:half + 1, n:n + 1], rate)
        return jnp.broadcast_to(rate, (1, HD))

    def mix(rate):
        return jnp.where(is0, 1.0 - rate, jnp.sqrt(1.0 - rate * rate))

    def chain_head(i):
        r0, r1 = rate_of(0, i), rate_of(1, i)
        f0, f1, both = mix(r0), mix(r1), r0 * r1
        for r in range(CUTS):
            k = i * CUTS + r
            rows_at = pl.ds(r * piece, piece)
            own = kv[kept, i, tail0 + r * piece:tail0 + (r + 1) * piece, :].astype(jnp.float32)
            with scope("waittail"):
                tail_copy(k, i, r).wait_recv()
            theirs = tail_in[i, rows_at, :].astype(jnp.float32)
            low = f0 * jnp.where(is0, own, theirs)
            high = r1 * low + f1 * jnp.where(is0, theirs, own)

            @pl.when(c > 0)
            def _():
                with scope("waitchain"):
                    chain_copy(k, i, r).wait_recv()

            state = s_in[i, rows_at, :].astype(jnp.float32)
            s_out[i, rows_at, :] = (both * state + high).astype(jnp.bfloat16)

            @pl.when(c < last)
            def _():
                chain_copy(k, i, r).start()

            later = r0 * state + low
            m_out[i, rows_at, :] = jnp.where(is0, later, state).astype(jnp.bfloat16)

            @pl.when(c > 0)
            def _():
                moved_copy(k, i, r).start()

            mem[kept, i, rows_at, :] = jnp.where(is0, state, later).astype(jnp.bfloat16)

    def frame_rows():
        total = frames.shape[1]
        wide = jnp.broadcast_to(frames[...], (8, total))
        ahead = pltpu.roll(wide, HALF, 1)
        behind = pltpu.roll(wide, total - (rows - HALF), 1)
        place = lax.broadcasted_iota(jnp.int32, wide.shape, 1)
        ext = jnp.where(is0, ahead, behind)
        least = jnp.where(is0, HALF, 0)
        limit = jnp.where(is0, total + HALF, rows + HALF)
        ext = jnp.where((place >= least) & (place < limit), ext, outside_frame)
        for g in range(groups):
            fr[g] = ext[:, g * GROUP:(g + 1) * GROUP].astype(jnp.float32)

    def local_group(g):
        at = pl.ds(g * GROUP, GROUP)
        key_frame = jnp.broadcast_to(fr[g][0:1, :], (GROUP, GROUP))
        same = (
            lax.broadcasted_iota(jnp.int32, (GROUP, GROUP), 0) // WIN
            == lax.broadcasted_iota(jnp.int32, (GROUP, GROUP), 1) // WIN
        )
        allowed = same & (key_frame <= key_frame.T)
        scores = [
            lax.dot_general(
                q[i, at, :], kv[0, i, at, :],
                (((1,), (1,)), ((), ())), preferred_element_type=jnp.float32,
            )
            for i in range(heads)
        ]
        weights = [jnp.where(allowed, jnp.exp2(score * score_factor), 0.0) for score in scores]
        values = [
            jnp.dot(weights[i].astype(jnp.bfloat16), kv[1, i, at, :], preferred_element_type=jnp.float32)
            for i in range(heads)
        ]
        for i in range(heads):
            den[i, at, :] = weights[i]
            num[i, at, :] = values[i]

    spots = [(i, n * 2 * GROUP, 2 * GROUP) for i in range(heads - 1) for n in range(rows // (2 * GROUP))]
    spots += [(heads - 1, n * GROUP, GROUP) for n in range(rows // GROUP)]
    sides, crosses, relays = [], [], []
    for j, (i, first, count) in enumerate(spots):
        at = pl.ds(first, count)
        mine = att.at[me, i, at]
        sides.append(remote(mine, mine, a_send, a_recv, {"mp": sib}))
        across, passed = [], []
        for o in range(1, chips):
            to = (me + 2 * o) % n_mp
            theirs = att.at[(me + n_mp - 2 * o) % n_mp, i, at]
            across.append(remote(mine, mine, c_send, c_recv.at[j, o - 1], {"mp": to}))
            passed.append(remote(theirs, theirs, r_send, r_recv.at[max(j - len(spots) + rows // GROUP + 1, 0)], {"mp": sib}))
        crosses.append(across)
        relays.append(passed)

    start = phase * (rows // WIN)

    def memory_groups(i, members):
        scores, flagged = [], []
        for g in members:
            window = start + g * (GROUP // WIN)
            row = lax.broadcasted_iota(jnp.int32, (GROUP, MEM), 0)
            flags = opened[0, window + GROUP // WIN]
            for n in range(GROUP // WIN - 1, -1, -1):
                flags = jnp.where(row < HALF + n * WIN, opened[0, window + n], flags)
            flagged.append(flags == 1)
            scores.append(lax.dot_general(
                q[i, HALF + g * GROUP:HALF + (g + 1) * GROUP, :], mem[0, i],
                (((1,), (1,)), ((), ())), preferred_element_type=jnp.float32,
            ))
        weights = [
            jnp.where(flags, jnp.exp2(score * score_factor), 0.0) for score, flags in zip(scores, flagged)
        ]
        values = [
            jnp.dot(weight.astype(jnp.bfloat16), mem[1, i], preferred_element_type=jnp.float32)
            for weight in weights
        ]
        for g, weight, value in zip(members, weights, values):
            at = slice(HALF + g * GROUP, HALF + (g + 1) * GROUP)
            total = den[i, at, :]
            for j in range(MEM // HD):
                total = total + weight[:, j * HD:(j + 1) * HD]
            denom = jnp.sum(total, axis=-1, keepdims=True)
            att[me, i, g * GROUP:(g + 1) * GROUP, :] = ((num[i, at, :] + value) / denom).astype(jnp.bfloat16)

    def memory_head(i):
        with scope("waitmem"):
            remote(m_out.at[i], mem.at[kept, i], m_send, m_recv.at[i], {"phase": other}).wait_recv()
        with scope("mem"):
            for base in range(0, rows, 2 * GROUP):
                memory_groups(i, [base // GROUP, base // GROUP + 1])
                for j, (which, first, count) in enumerate(spots):
                    if which == i and base <= first < base + 2 * GROUP:
                        for copy in crosses[j]:
                            copy.start()
                        sides[j].start()

    def relay_head(i, n):
        for at in range(i * per_head + n * per_head // 2, i * per_head + (n + 1) * per_head // 2):
            relay(at)

    end = heads * per_head
    plan = {}
    for kind, spots_of in enumerate(PLAN):
        for i, place in enumerate(spots_of):
            plan.setdefault(place, []).append((kind, i))

    def chain_at(place):
        kind, i = jnp.minimum(c, len(PLAN) - 1), jnp.int32(heads)
        for which, head in plan[place]:
            if head < heads:
                i = jnp.where(kind == which, head, i)

        @pl.when(i < heads)
        def _():
            with scope("chain%d" % place):
                chain_head(i)

    chain_at(0)
    with scope("head1"):
        columns(0, top, 0, wide)
    send_columns(chips - 1)
    with scope("head2"):
        columns(0, top, wide, 2 * wide)
    halo.start()
    chain_at(1)
    with scope("head3"):
        columns(0, top, 2 * wide, 3 * heads)
    send_columns(chips - 1)
    chain_at(2)
    relay_head(0, 0)
    relay_up(0, acrosses[0])
    with scope("local"):
        frame_rows()
        for g in range(1, groups - 1):
            local_group(g)
    send_columns(len(wo_copies))
    chain_at(3)

    @pl.when(c == 0)
    def _():
        for copy in each(moved_copy):
            copy.start()

    relay_head(0, 1)
    chain_at(4)
    with scope("local"):
        with scope("halo"):
            halo.wait_recv()
        local_group(0)
        local_group(groups - 1)
    relay_head(1, 0)
    chain_at(5)
    relay_head(1, 1)
    chain_at(6)
    relay_head(2, 0)
    memory_head(0)
    chain_at(7)
    relay_up(per_head, 2 * per_head + per_head // 2)
    relay_head(2, 1)
    memory_head(1)
    relay_up(2 * per_head + per_head // 2, heads * per_head)
    memory_head(2)

    own = pl.ds(pl.multiple_of(me * share, HD), share)

    def product(sources, which, first, count):
        left = jnp.concatenate([att[m, i, first:first + count, :] for m in sources for i in which], axis=1)
        right = jnp.concatenate([wo[m, i * HD:(i + 1) * HD, :] for m in sources for i in which], axis=0)
        return jnp.dot(left, right, preferred_element_type=jnp.float32)

    def add(sources, which, scope_name):
        with scope(scope_name):
            for first in range(0, rows, 2 * GROUP):
                at = slice(first, first + 2 * GROUP)
                acc[at, :] = acc[at, :] + product(sources, which, first, 2 * GROUP)

    def cross(j):
        for o in range(chips - 1):
            with scope("waitcross"):
                crosses[j][o].wait_recv()
            relays[j][o].start()

    def arrived(lot, which):
        with scope("waitrelay"):
            remote(lot, lot, r_send, r_recv.at[which], {"mp": sib}).wait_recv()

    def far_weights(i):
        with scope("waitwo"):
            lot = wo.at[pl.ds(0, chips - 1), pl.ds(0, HD)]
            remote(lot, lot, wd_send, wr_recv.at[i], {"phase": other}).wait_recv()

    order = [[j for j, spot in enumerate(spots) if spot[0] == i] for i in range(heads)]
    wo_own.wait()
    with scope("own"):
        for first in range(0, rows, 2 * GROUP):
            at = slice(first, first + 2 * GROUP)
            acc[at, :] = x[at, own].astype(jnp.float32) + product([me], range(heads), first, 2 * GROUP)
    early = range(heads - 1)
    for j in order[0]:
        cross(j)
    with scope("waitside"):
        wo_side.wait_recv()
        remote(att.at[me], att.at[me], a_send, a_recv, {"mp": sib}).wait_recv()
    add([sib], range(heads), "near")
    for i in early[1:]:
        for j in order[i]:
            cross(j)
    for i in early:
        far_weights(i)
    add(far[0::2], early, "direct")
    final = order[heads - 1]
    for j in final[:-1]:
        cross(j)
    arrived(att.at[pl.ds(0, chips - 1), pl.ds(0, heads - 1)], 0)
    add(far[1::2], early, "passed")
    far_weights(heads - 1)
    cross(final[-1])
    for n, j in enumerate(final):
        first, count = spots[j][1], spots[j][2]
        arrived(att.at[pl.ds(0, chips - 1), heads - 1, pl.ds(first, count)], 1 + n)
        if n % 2:
            with scope("fin"):
                at = slice(first - count, first + count)
                out[at, :] = (
                    acc[at, :] + product(far, [heads - 1], first - count, 2 * count)
                ).astype(jnp.bfloat16)

    with scope("sends"):
        tail_all = kv.at[sent, :, pl.ds(tail0, MEM)]
        wo_all = wo.at[pl.ds(0, chips - 1)]
        att_all = att.at[pl.ds(0, chips - 1)]
        for src, send, recv, where in (
            (tail_all, y_send, y_recv.at[0], {"phase": other}),
            (m_out, m_send, m_recv.at[0], {"phase": other}),
            (wo_all, wo_send, wo_recv.at[0], {"mp": sib}),
            (att.at[me], a_send, a_recv, {"mp": sib}),
            (att_all, c_send, c_recv.at[0, 0], {"mp": sib}),
            (att_all, r_send, r_recv.at[0], {"mp": sib}),
        ):
            remote(src, src, send, recv, where).wait_send()
        halo.wait_send()
        wo_side.wait_send()

        @pl.when(c < last)
        def _():
            remote(s_out, s_in, z_send, z_recv.at[0], {"phase": other}).wait_send()

        @pl.when(c > 0)
        def _():
            remote(wo_all, wo_all, wd_send, wr_recv.at[0], {"phase": other}).wait_send()

        @pl.when(c == last - 1)
        def _():
            lot = wo.at[pl.ds(0, chips - 1), pl.ds(0, cols - block)]
            remote(lot, lot, wu_send, wr_recv.at[0], {"phase": other}).wait_send()

        @pl.when(c == last)
        def _():
            lot = wo.at[pl.ds(0, chips - 1), pl.ds(0, block)]
            remote(lot, lot, wu_send, wr_recv.at[0], {"phase": other}).wait_send()


def local(n_span, n_mp, latents, w_qkv, w_out, decay, frame_ids, memory_mask):
    rows, width = latents.shape
    cols = w_qkv.shape[2]
    heads = cols // HD
    share = width // n_mp
    ext = -(-(rows + WIN) // GROUP) * GROUP
    groups = ext // GROUP
    others = max(n_mp // 2 - 1, 1)
    chunks = 2 * others * heads
    pieces = heads * CUTS
    spots = (heads - 1) * (rows // (2 * GROUP)) + rows // GROUP
    hbm_spec = pl.BlockSpec(memory_space=pltpu.HBM)
    dma = pltpu.SemaphoreType.DMA
    bf16, f32 = jnp.bfloat16, jnp.float32
    flops = 2 * rows * width * 4 * cols
    inputs = (
        latents, jnp.transpose(w_qkv, (1, 0, 2)), w_out,
        decay.reshape(decay.shape[1:]), frame_ids, memory_mask,
    )
    return pl.pallas_call(
        functools.partial(body, (n_span, n_mp, rows, width, cols)),
        out_shape=jax.ShapeDtypeStruct((rows, share), bf16),
        in_specs=[hbm_spec] * 6,
        out_specs=pl.BlockSpec(memory_space=pltpu.VMEM),
        scratch_shapes=[
            pltpu.VMEM(decay.shape[1:], f32),
            pltpu.VMEM(frame_ids.shape, jnp.int32),
            pltpu.SMEM(memory_mask.shape, jnp.int32),
            pltpu.VMEM((rows, width), bf16),
            pltpu.VMEM((width, 3 * cols), bf16),
            pltpu.VMEM((n_mp, cols, share), bf16),
            pltpu.VMEM((2, heads, ext, HD), bf16),
            pltpu.VMEM((heads, ext, HD), bf16),
            pltpu.VMEM((heads, ext, HD), f32),
            pltpu.VMEM((heads, ext, HD), f32),
            pltpu.VMEM((n_mp, heads, rows, HD), bf16),
            pltpu.VMEM((rows, share), f32),
            pltpu.VMEM((groups, 8, GROUP), f32),
            pltpu.VMEM((heads, MEM, HD), bf16),
            pltpu.VMEM((heads, MEM, HD), bf16),
            pltpu.VMEM((heads, MEM, HD), bf16),
            pltpu.VMEM((heads, MEM, HD), bf16),
            pltpu.VMEM((2, heads, MEM, HD), bf16),
            dma((KPARTS + 8,)),
            dma, dma,
            dma, dma((chunks,)), dma, dma, dma((heads,)),
            dma, dma((pieces,)),
            dma, dma((pieces,)),
            dma, dma((heads,)),
            dma, dma,
            dma, dma,
            dma, dma((spots, others)),
            dma, dma((1 + rows // GROUP,)),
        ],
        compiler_params=pltpu.CompilerParams(
            collective_id=0, has_side_effects=True, vmem_limit_bytes=40 * 1024 * 1024
        ),
        cost_estimate=pl.CostEstimate(flops=flops, bytes_accessed=12 << 20, transcendentals=1 << 20),
        name="refiner",
    )(*[pltpu.with_memory_space_constraint(a, pltpu.HBM) for a in inputs])


def solution(mesh):
    return jax.shard_map(
        functools.partial(local, mesh.shape["span"], mesh.shape["mp"]),
        mesh=mesh,
        in_specs=(
            P(("span", "phase"), None),
            P(None, None, "mp"),
            P("mp", None),
            P("span", None, "mp"),
            P("span", None),
            P("span", None),
        ),
        out_specs=P(("span", "phase"), "mp"),
        check_vma=False,
    )
```

```python
import contextlib
import functools
import math

import jax
import jax.numpy as jnp
from jax import lax
from jax.experimental import pallas as pl
from jax.experimental.pallas import tpu as pltpu
from jax.sharding import PartitionSpec as P

HD = 128
WIN = 64
MEM = 256
HALF = WIN // 2
GROUP = 128
CUTS = 4
DIRECT = 2
KPARTS = 2
PLAN = ((0, 1, 3), (2, 4, 5), (4, 5, 7), (4, 6, 7))
MESH = pl.DeviceIdType.MESH

outside_frame = 1048576
epsilon = 1e-06
score_factor = HD ** (-0.5) * math.log2(math.e)


@contextlib.contextmanager
def scope(name):
    yield


def remote(src, dst, send, recv, where):
    return pltpu.make_async_remote_copy(
        src_ref=src, dst_ref=dst, send_sem=send, recv_sem=recv,
        device_id=where, device_id_type=MESH,
    )


def body(
    sizes, x_hbm, w_hbm, wo_hbm, decay_hbm, frames_hbm, opened_hbm, out,
    decay, frames, opened, x, w, wo, kv, q, num, den, att, acc, fr, tail_in, s_in, s_out, m_out, mem,
    load_sem, ws_send, ws_recv, wo_send, wo_recv, wd_send, wu_send, wr_recv, y_send, y_recv, z_send, z_recv, m_send, m_recv,
    h_send, h_recv, a_send, a_recv, c_send, c_recv, r_send, r_recv,
):
    n_span, n_mp, rows, width, cols = sizes
    heads = cols // HD
    share = width // n_mp
    groups = kv.shape[2] // GROUP
    c = lax.axis_index("span")
    me = lax.axis_index("mp")
    phase = lax.axis_index("phase")
    is0 = phase == 0
    other = 1 - phase
    kept, sent = phase, 1 - phase
    sib = me + 1 - 2 * (me % 2)
    chips = n_mp // 2
    top = rows - MEM
    tail0 = HALF + top
    piece = MEM // CUTS
    last = n_span - 1

    barrier = pltpu.get_barrier_semaphore()
    for o in range(1, n_mp):
        pl.semaphore_signal(barrier, inc=1, device_id={"mp": (me + o) % n_mp}, device_id_type=MESH)
    pl.semaphore_signal(barrier, inc=1, device_id={"phase": other}, device_id_type=MESH)

    @pl.when(c > 0)
    def _():
        pl.semaphore_signal(barrier, inc=1, device_id={"span": c - 1}, device_id_type=MESH)

    @pl.when(c < last)
    def _():
        pl.semaphore_signal(barrier, inc=1, device_id={"span": c + 1}, device_id_type=MESH)

    def load(i, src, dst):
        copy = pltpu.make_async_copy(src, dst, load_sem.at[i])
        copy.start()
        return copy

    deep = width // KPARTS
    for n in range(KPARTS):
        at = pl.ds(n * deep, deep)
        load(n, x_hbm.at[pl.ds(top, MEM), at], x.at[pl.ds(top, MEM), at])
        load(n, w_hbm.at[1 + sent, at, pl.ds(0, HD)], w.at[at, pl.ds(0, HD)])
    both_parts = w.at[pl.ds(0, deep), pl.ds(0, MEM + HD)]
    w_sent = load(KPARTS, w_hbm.at[1 + sent, :, pl.ds(HD, cols - HD)], w.at[:, pl.ds(HD, cols - HD)])
    w_kept = load(KPARTS + 1, w_hbm.at[1 + kept], w.at[:, pl.ds(cols, cols)])
    w_query = load(KPARTS + 2, w_hbm.at[0], w.at[:, pl.ds(2 * cols, cols)])
    small = [
        load(KPARTS + 3, decay_hbm, decay), load(KPARTS + 4, frames_hbm, frames), load(KPARTS + 5, opened_hbm, opened),
    ]
    x_head = load(KPARTS + 6, x_hbm.at[pl.ds(0, top)], x.at[pl.ds(0, top)])
    wo_own = load(KPARTS + 7, wo_hbm.at[:, pl.ds(pl.multiple_of(me * share, HD), share)], wo.at[me])

    zero_rows = kv.shape[2] - (HALF + rows + HALF)
    kv[:, :, HALF + rows + HALF:, :] = jnp.zeros((2, heads, zero_rows, HD), jnp.bfloat16)
    q[:, HALF + rows:, :] = jnp.zeros((heads, q.shape[1] - HALF - rows, HD), jnp.bfloat16)
    q[:, :HALF, :] = jnp.zeros((heads, HALF, HD), jnp.bfloat16)
    blank = pl.multiple_of(phase * (HALF + rows), HALF)
    kv[:, :, pl.ds(blank, HALF), :] = jnp.zeros((2, heads, HALF, HD), jnp.bfloat16)

    @pl.when(c == 0)
    def _():
        s_in[...] = jnp.zeros(s_in.shape, s_in.dtype)

    block = HD // 2
    parity = (c + phase) % 2

    def columns_of(m):
        return pl.ds(pl.multiple_of(m * share, HD), share)

    wo_copies, wo_downs, wo_ups, wo_acrosses, far = [], [], {}, [], []
    acrosses = range(chips - 1, 2 * (chips - 1))
    for o in range(1, chips):
        for near in (me, sib):
            far.append((near + n_mp - 2 * o) % n_mp)
    for i in range(heads):
        part = pl.ds(pl.multiple_of(i * HD + parity * block, block), block)
        for o in range(1, chips):
            for near in (me, sib):
                to, source = (near + 2 * o) % n_mp, (near + n_mp - 2 * o) % n_mp
                at = len(wo_copies)
                wo_copies.append(remote(
                    wo_hbm.at[part, columns_of(to)], wo.at[me, part],
                    wo_send, wo_recv.at[at], {"mp": to},
                ))
                held = wo.at[source, part]
                wo_downs.append(remote(held, held, wd_send, wr_recv.at[i], {"span": (c + last) % n_span}))
                if at in acrosses:
                    wo_acrosses.append(remote(held, held, wu_send, wr_recv.at[i], {"phase": other}))
                else:
                    wo_ups[at] = remote(held, held, wu_send, wr_recv.at[i], {"span": (c + 1) % n_span})
    wo_side = remote(wo_hbm.at[:, columns_of(sib)], wo.at[me], ws_send, ws_recv, {"mp": sib})
    per_head = len(far)

    def relay(at):
        with scope("relay"):
            wo_copies[at].wait_recv()

        @pl.when(c > 0)
        def _():
            wo_downs[at].start()

        if at in acrosses:
            @pl.when(c == last)
            def _():
                wo_acrosses[at - acrosses[0]].start()

    def relay_up(first, end):
        @pl.when(c == last - 1)
        def _():
            for at in range(first, end):
                wo_ups[at].start()

    def unit(part, flag):
        scale = lax.rsqrt(jnp.mean(part * part, axis=-1, keepdims=True) + epsilon)
        if flag is not None:
            scale = jnp.where(flag, scale, 1.0)
        return (part * scale).astype(jnp.bfloat16)

    def project(first, count, column, size):
        return jnp.dot(
            x[first:first + count, :], w[:, column:column + size],
            preferred_element_type=jnp.float32,
        )

    def tail_copy(k, i, r):
        return remote(
            kv.at[sent, i, pl.ds(tail0 + r * piece, piece)], tail_in.at[i, pl.ds(r * piece, piece)],
            y_send, y_recv.at[k], {"phase": other},
        )

    def chain_copy(k, i, r):
        at = pl.ds(r * piece, piece)
        return remote(s_out.at[i, at], s_in.at[i, at], z_send, z_recv.at[k], {"span": (c + 1) % n_span})

    def moved_copy(k, i, r):
        at = pl.ds(r * piece, piece)
        return remote(m_out.at[i, at], mem.at[kept, i, at], m_send, m_recv.at[i], {"phase": other})

    def each(make):
        return [make(i * CUTS + r, i, r) for i in range(heads) for r in range(CUTS)]

    tails = each(tail_copy)

    def keep(raw, first, count, n, at):
        part = raw[:, at * HD:(at + 1) * HD]
        rows_at = slice(HALF + first, HALF + first + count)
        if n >= 2 * heads:
            q[n - 2 * heads, rows_at, :] = unit(part, None)
        else:
            which = sent if n < heads else kept
            kv[which, n % heads, rows_at, :] = unit(part, which == 0)

    def columns(first, count, n, end):
        raw = project(first, count, n * HD, (end - n) * HD)
        for at in range(end - n):
            keep(raw, first, count, n + at, at)

    def send_tail(i):
        for r in range(CUTS):
            tails[i * CUTS + r].start()

    begun = 0

    def send_columns(count):
        nonlocal begun
        for copy in wo_copies[begun:begun + count]:
            copy.start()
        begun += count

    raw = None
    for n in range(KPARTS):
        with scope("load%d" % n):
            pltpu.make_async_copy(both_parts, both_parts, load_sem.at[n]).wait()
        if n == KPARTS - 1:
            with scope("bar"):
                pl.semaphore_wait(barrier, n_mp + 1 + (c + n_span - 1) // n_span - (c + 1) // n_span)
            send_columns(2 * (chips - 1))
        with scope("sent%d" % n):
            for start in range(n * deep, (n + 1) * deep, deep // 2):
                at = slice(start, start + deep // 2)
                step = jnp.dot(x[top:, at], w[at, :HD], preferred_element_type=jnp.float32)
                raw = step if raw is None else raw + step
    with scope("unit"):
        keep(raw, top, MEM, 0, 0)
    send_tail(0)
    wo_side.start()
    for copy in small:
        copy.wait()
    wide = -(-(3 * heads - 1) // 2)
    with scope("loadk"):
        w_sent.wait()
        w_kept.wait()
    with scope("tail1"):
        columns(top, MEM, 1, 1 + wide)
    send_tail(1)
    send_columns(chips - 1)
    with scope("loadq"):
        w_query.wait()
    with scope("tail2"):
        columns(top, MEM, 1 + wide, 3 * heads)
    for i in range(2, heads):
        send_tail(i)
    with scope("loadx"):
        x_head.wait()
    halo_from = pl.multiple_of(HALF + other * (rows - HALF), HALF)
    halo = remote(
        kv.at[:, :, pl.ds(halo_from, HALF)], kv.at[:, :, pl.ds(blank, HALF)],
        h_send, h_recv, {"phase": other},
    )

    def rate_of(half, i):
        rate = decay[half:half + 1, 0:1]
        for n in range(1, heads):
            rate = jnp.where(i == n, decay[half:half + 1, n:n + 1], rate)
        return jnp.broadcast_to(rate, (1, HD))

    def mix(rate):
        return jnp.where(is0, 1.0 - rate, jnp.sqrt(1.0 - rate * rate))

    def chain_head(i):
        r0, r1 = rate_of(0, i), rate_of(1, i)
        f0, f1, both = mix(r0), mix(r1), r0 * r1
        for r in range(CUTS):
            k = i * CUTS + r
            rows_at = pl.ds(r * piece, piece)
            own = kv[kept, i, tail0 + r * piece:tail0 + (r + 1) * piece, :].astype(jnp.float32)
            with scope("waittail"):
                tail_copy(k, i, r).wait_recv()
            theirs = tail_in[i, rows_at, :].astype(jnp.float32)
            low = f0 * jnp.where(is0, own, theirs)
            high = r1 * low + f1 * jnp.where(is0, theirs, own)

            @pl.when(c > 0)
            def _():
                with scope("waitchain"):
                    chain_copy(k, i, r).wait_recv()

            state = s_in[i, rows_at, :].astype(jnp.float32)
            s_out[i, rows_at, :] = (both * state + high).astype(jnp.bfloat16)

            @pl.when(c < last)
            def _():
                chain_copy(k, i, r).start()

            later = r0 * state + low
            m_out[i, rows_at, :] = jnp.where(is0, later, state).astype(jnp.bfloat16)

            @pl.when(c > 0)
            def _():
                moved_copy(k, i, r).start()

            mem[kept, i, rows_at, :] = jnp.where(is0, state, later).astype(jnp.bfloat16)

    def frame_rows():
        total = frames.shape[1]
        wide = jnp.broadcast_to(frames[...], (8, total))
        ahead = pltpu.roll(wide, HALF, 1)
        behind = pltpu.roll(wide, total - (rows - HALF), 1)
        place = lax.broadcasted_iota(jnp.int32, wide.shape, 1)
        ext = jnp.where(is0, ahead, behind)
        least = jnp.where(is0, HALF, 0)
        limit = jnp.where(is0, total + HALF, rows + HALF)
        ext = jnp.where((place >= least) & (place < limit), ext, outside_frame)
        for g in range(groups):
            fr[g] = ext[:, g * GROUP:(g + 1) * GROUP].astype(jnp.float32)

    def local_group(g):
        at = pl.ds(g * GROUP, GROUP)
        key_frame = jnp.broadcast_to(fr[g][0:1, :], (GROUP, GROUP))
        same = (
            lax.broadcasted_iota(jnp.int32, (GROUP, GROUP), 0) // WIN
            == lax.broadcasted_iota(jnp.int32, (GROUP, GROUP), 1) // WIN
        )
        allowed = same & (key_frame <= key_frame.T)
        scores = [
            lax.dot_general(
                q[i, at, :], kv[0, i, at, :],
                (((1,), (1,)), ((), ())), preferred_element_type=jnp.float32,
            )
            for i in range(heads)
        ]
        weights = [jnp.where(allowed, jnp.exp2(score * score_factor), 0.0) for score in scores]
        values = [
            jnp.dot(weights[i].astype(jnp.bfloat16), kv[1, i, at, :], preferred_element_type=jnp.float32)
            for i in range(heads)
        ]
        for i in range(heads):
            den[i, at, :] = weights[i]
            num[i, at, :] = values[i]

    spots = [(i, n * 2 * GROUP, 2 * GROUP) for i in range(heads - 1) for n in range(rows // (2 * GROUP))]
    spots += [(heads - 1, n * GROUP, GROUP) for n in range(rows // GROUP)]
    sides, crosses, relays = [], [], []
    for j, (i, first, count) in enumerate(spots):
        at = pl.ds(first, count)
        mine = att.at[me, i, at]
        sides.append(remote(mine, mine, a_send, a_recv, {"mp": sib}))
        across, passed = [], []
        for o in range(1, chips):
            to = (me + 2 * o) % n_mp
            theirs = att.at[(me + n_mp - 2 * o) % n_mp, i, at]
            across.append(remote(mine, mine, c_send, c_recv.at[j, o - 1], {"mp": to}))
            passed.append(remote(theirs, theirs, r_send, r_recv.at[max(j - len(spots) + rows // GROUP + 1, 0)], {"mp": sib}))
        crosses.append(across)
        relays.append(passed)

    direct = {}
    for n, j in enumerate(range(len(spots) - DIRECT, len(spots))):
        i, first, count = spots[j]
        mine = att.at[me, i, pl.ds(first, count)]
        direct[j] = [
            remote(mine, mine, r_send, r_recv.at[1 + rows // GROUP - DIRECT + n], {"mp": (sib + 2 * o) % n_mp})
            for o in range(1, chips)
        ]
    even = me % 2 == 0

    start = phase * (rows // WIN)

    def memory_groups(i, members):
        scores, flagged = [], []
        for g in members:
            window = start + g * (GROUP // WIN)
            row = lax.broadcasted_iota(jnp.int32, (GROUP, MEM), 0)
            flags = opened[0, window + GROUP // WIN]
            for n in range(GROUP // WIN - 1, -1, -1):
                flags = jnp.where(row < HALF + n * WIN, opened[0, window + n], flags)
            flagged.append(flags == 1)
            scores.append(lax.dot_general(
                q[i, HALF + g * GROUP:HALF + (g + 1) * GROUP, :], mem[0, i],
                (((1,), (1,)), ((), ())), preferred_element_type=jnp.float32,
            ))
        weights = [
            jnp.where(flags, jnp.exp2(score * score_factor), 0.0) for score, flags in zip(scores, flagged)
        ]
        values = [
            jnp.dot(weight.astype(jnp.bfloat16), mem[1, i], preferred_element_type=jnp.float32)
            for weight in weights
        ]
        for g, weight, value in zip(members, weights, values):
            at = slice(HALF + g * GROUP, HALF + (g + 1) * GROUP)
            total = den[i, at, :]
            for j in range(MEM // HD):
                total = total + weight[:, j * HD:(j + 1) * HD]
            denom = jnp.sum(total, axis=-1, keepdims=True)
            att[me, i, g * GROUP:(g + 1) * GROUP, :] = ((num[i, at, :] + value) / denom).astype(jnp.bfloat16)

    def memory_head(i):
        with scope("waitmem"):
            remote(m_out.at[i], mem.at[kept, i], m_send, m_recv.at[i], {"phase": other}).wait_recv()
        with scope("mem"):
            for base in range(0, rows, 2 * GROUP):
                memory_groups(i, [base // GROUP, base // GROUP + 1])
                for j, (which, first, count) in enumerate(spots):
                    if which == i and base <= first < base + 2 * GROUP:
                        for copy in crosses[j]:
                            copy.start()
                        if j in direct:
                            @pl.when(even)
                            def _(copies=direct[j]):
                                for copy in copies:
                                    copy.start()
                        sides[j].start()

    def relay_head(i, n):
        for at in range(i * per_head + n * per_head // 2, i * per_head + (n + 1) * per_head // 2):
            relay(at)

    end = heads * per_head
    plan = {}
    for kind, spots_of in enumerate(PLAN):
        for i, place in enumerate(spots_of):
            plan.setdefault(place, []).append((kind, i))

    def chain_at(place):
        kind, i = jnp.minimum(c, len(PLAN) - 1), jnp.int32(heads)
        for which, head in plan[place]:
            if head < heads:
                i = jnp.where(kind == which, head, i)

        @pl.when(i < heads)
        def _():
            with scope("chain%d" % place):
                chain_head(i)

    chain_at(0)
    with scope("head1"):
        columns(0, top, 0, wide)
    send_columns(chips - 1)
    chain_at(1)
    with scope("head2"):
        columns(0, top, wide, 2 * wide)
    halo.start()

    @pl.when(c == 0)
    def _():
        for r in range(CUTS):
            moved_copy(r, 0, r).start()

    chain_at(2)
    with scope("head3"):
        columns(0, top, 2 * wide, 3 * heads)
    send_columns(chips - 1)
    relay_head(0, 0)
    relay_up(0, acrosses[0])
    with scope("local"):
        frame_rows()
        for g in range(1, groups - 1):
            local_group(g)
    send_columns(len(wo_copies))
    chain_at(3)

    @pl.when(c == 0)
    def _():
        for i in range(1, heads):
            for r in range(CUTS):
                moved_copy(i * CUTS + r, i, r).start()

    relay_head(0, 1)
    chain_at(4)
    with scope("local"):
        with scope("halo"):
            halo.wait_recv()
        local_group(0)
        local_group(groups - 1)
    relay_head(1, 0)
    chain_at(5)
    relay_head(1, 1)
    chain_at(6)
    memory_head(0)
    chain_at(7)
    relay_head(2, 0)
    relay_up(per_head, 2 * per_head + per_head // 2)
    relay_head(2, 1)
    memory_head(1)
    relay_up(2 * per_head + per_head // 2, heads * per_head)
    memory_head(2)

    own = pl.ds(pl.multiple_of(me * share, HD), share)

    def product(sources, which, first, count):
        left = jnp.concatenate([att[m, i, first:first + count, :] for m in sources for i in which], axis=1)
        right = jnp.concatenate([wo[m, i * HD:(i + 1) * HD, :] for m in sources for i in which], axis=0)
        return jnp.dot(left, right, preferred_element_type=jnp.float32)

    def add(sources, which, scope_name):
        with scope(scope_name):
            for first in range(0, rows, 2 * GROUP):
                at = slice(first, first + 2 * GROUP)
                acc[at, :] = acc[at, :] + product(sources, which, first, 2 * GROUP)

    def cross(j):
        for o in range(chips - 1):
            with scope("waitcross"):
                crosses[j][o].wait_recv()
            if j in direct:
                @pl.when(jnp.logical_not(even))
                def _(copy=relays[j][o]):
                    copy.start()
            else:
                relays[j][o].start()

    def arrived(lot, which):
        with scope("waitrelay"):
            remote(lot, lot, r_send, r_recv.at[which], {"mp": sib}).wait_recv()

    def far_weights(i):
        with scope("waitwo"):
            lot = wo.at[pl.ds(0, chips - 1), pl.ds(0, HD)]
            remote(lot, lot, wd_send, wr_recv.at[i], {"phase": other}).wait_recv()

    order = [[j for j, spot in enumerate(spots) if spot[0] == i] for i in range(heads)]
    wo_own.wait()
    with scope("own"):
        for first in range(0, rows, 2 * GROUP):
            at = slice(first, first + 2 * GROUP)
            acc[at, :] = x[at, own].astype(jnp.float32) + product([me], range(heads), first, 2 * GROUP)
    early = range(heads - 1)
    for j in order[0]:
        cross(j)
    with scope("waitside"):
        wo_side.wait_recv()
        remote(att.at[me], att.at[me], a_send, a_recv, {"mp": sib}).wait_recv()
    add([sib], range(heads), "near")
    for i in early[1:]:
        for j in order[i]:
            cross(j)
    for i in early:
        far_weights(i)
    add(far[0::2], early, "direct")
    final = order[heads - 1]
    for j in final:
        cross(j)
    arrived(att.at[pl.ds(0, chips - 1), pl.ds(0, heads - 1)], 0)
    add(far[1::2], early, "passed")
    far_weights(heads - 1)
    for n, j in enumerate(final):
        first, count = spots[j][1], spots[j][2]
        arrived(att.at[pl.ds(0, chips - 1), heads - 1, pl.ds(first, count)], 1 + n)
        if n % 2:
            with scope("fin"):
                at = slice(first - count, first + count)
                out[at, :] = (
                    acc[at, :] + product(far, [heads - 1], first - count, 2 * count)
                ).astype(jnp.bfloat16)

    with scope("sends"):
        tail_all = kv.at[sent, :, pl.ds(tail0, MEM)]
        wo_all = wo.at[pl.ds(0, chips - 1)]
        att_all = att.at[pl.ds(0, chips - 1)]
        for src, send, recv, where in (
            (tail_all, y_send, y_recv.at[0], {"phase": other}),
            (m_out, m_send, m_recv.at[0], {"phase": other}),
            (wo_all, wo_send, wo_recv.at[0], {"mp": sib}),
            (att.at[me], a_send, a_recv, {"mp": sib}),
            (att_all, c_send, c_recv.at[0, 0], {"mp": sib}),
            (att_all, r_send, r_recv.at[0], {"mp": sib}),
        ):
            remote(src, src, send, recv, where).wait_send()
        halo.wait_send()
        wo_side.wait_send()

        @pl.when(c < last)
        def _():
            remote(s_out, s_in, z_send, z_recv.at[0], {"phase": other}).wait_send()

        @pl.when(c > 0)
        def _():
            remote(wo_all, wo_all, wd_send, wr_recv.at[0], {"phase": other}).wait_send()

        @pl.when(c == last - 1)
        def _():
            lot = wo.at[pl.ds(0, chips - 1), pl.ds(0, cols - block)]
            remote(lot, lot, wu_send, wr_recv.at[0], {"phase": other}).wait_send()

        @pl.when(c == last)
        def _():
            lot = wo.at[pl.ds(0, chips - 1), pl.ds(0, block)]
            remote(lot, lot, wu_send, wr_recv.at[0], {"phase": other}).wait_send()


def local(n_span, n_mp, latents, w_qkv, w_out, decay, frame_ids, memory_mask):
    rows, width = latents.shape
    cols = w_qkv.shape[2]
    heads = cols // HD
    share = width // n_mp
    ext = -(-(rows + WIN) // GROUP) * GROUP
    groups = ext // GROUP
    others = max(n_mp // 2 - 1, 1)
    chunks = 2 * others * heads
    pieces = heads * CUTS
    spots = (heads - 1) * (rows // (2 * GROUP)) + rows // GROUP
    hbm_spec = pl.BlockSpec(memory_space=pltpu.HBM)
    dma = pltpu.SemaphoreType.DMA
    bf16, f32 = jnp.bfloat16, jnp.float32
    flops = 2 * rows * width * 4 * cols
    inputs = (
        latents, jnp.transpose(w_qkv, (1, 0, 2)), w_out,
        decay.reshape(decay.shape[1:]), frame_ids, memory_mask,
    )
    return pl.pallas_call(
        functools.partial(body, (n_span, n_mp, rows, width, cols)),
        out_shape=jax.ShapeDtypeStruct((rows, share), bf16),
        in_specs=[hbm_spec] * 6,
        out_specs=pl.BlockSpec(memory_space=pltpu.VMEM),
        scratch_shapes=[
            pltpu.VMEM(decay.shape[1:], f32),
            pltpu.VMEM(frame_ids.shape, jnp.int32),
            pltpu.SMEM(memory_mask.shape, jnp.int32),
            pltpu.VMEM((rows, width), bf16),
            pltpu.VMEM((width, 3 * cols), bf16),
            pltpu.VMEM((n_mp, cols, share), bf16),
            pltpu.VMEM((2, heads, ext, HD), bf16),
            pltpu.VMEM((heads, ext, HD), bf16),
            pltpu.VMEM((heads, ext, HD), f32),
            pltpu.VMEM((heads, ext, HD), f32),
            pltpu.VMEM((n_mp, heads, rows, HD), bf16),
            pltpu.VMEM((rows, share), f32),
            pltpu.VMEM((groups, 8, GROUP), f32),
            pltpu.VMEM((heads, MEM, HD), bf16),
            pltpu.VMEM((heads, MEM, HD), bf16),
            pltpu.VMEM((heads, MEM, HD), bf16),
            pltpu.VMEM((heads, MEM, HD), bf16),
            pltpu.VMEM((2, heads, MEM, HD), bf16),
            dma((KPARTS + 8,)),
            dma, dma,
            dma, dma((chunks,)), dma, dma, dma((heads,)),
            dma, dma((pieces,)),
            dma, dma((pieces,)),
            dma, dma((heads,)),
            dma, dma,
            dma, dma,
            dma, dma((spots, others)),
            dma, dma((1 + rows // GROUP,)),
        ],
        compiler_params=pltpu.CompilerParams(
            collective_id=0, has_side_effects=True, vmem_limit_bytes=40 * 1024 * 1024
        ),
        cost_estimate=pl.CostEstimate(flops=flops, bytes_accessed=12 << 20, transcendentals=1 << 20),
        name="refiner",
    )(*[pltpu.with_memory_space_constraint(a, pltpu.HBM) for a in inputs])


def solution(mesh):
    return jax.shard_map(
        functools.partial(local, mesh.shape["span"], mesh.shape["mp"]),
        mesh=mesh,
        in_specs=(
            P(("span", "phase"), None),
            P(None, None, "mp"),
            P("mp", None),
            P("span", None, "mp"),
            P("span", None),
            P("span", None),
        ),
        out_specs=P(("span", "phase"), "mp"),
        check_vma=False,
    )
```

```python
import contextlib
import functools
import math

import jax
import jax.numpy as jnp
from jax import lax
from jax.experimental import pallas as pl
from jax.experimental.pallas import tpu as pltpu
from jax.sharding import PartitionSpec as P

HD = 128
WIN = 64
MEM = 256
HALF = WIN // 2
GROUP = 128
CUTS = 4
DIRECT = 2
ROW_PARTS = 2
PLAN = ((0, 1, 2), (2, 3, 5), (4, 5, 7), (4, 6, 7))
MESH = pl.DeviceIdType.MESH

outside_frame = 1048576
epsilon = 1e-06
score_factor = HD ** (-0.5) * math.log2(math.e)


@contextlib.contextmanager
def scope(name):
    yield


def remote(src, dst, send, recv, where):
    return pltpu.make_async_remote_copy(
        src_ref=src, dst_ref=dst, send_sem=send, recv_sem=recv,
        device_id=where, device_id_type=MESH,
    )


def body(
    sizes, x_hbm, w_hbm, wo_hbm, decay_hbm, frames_hbm, opened_hbm, out,
    decay, frames, opened, x, w, wo, kv, q, num, den, att, acc, fr, tail_in, s_in, s_out, m_out, mem,
    load_sem, ws_send, ws_recv, wo_send, wo_recv, wd_send, wu_send, wr_recv, y_send, y_recv, z_send, z_recv, m_send, m_recv,
    h_send, h_recv, a_send, a_recv, c_send, c_recv, r_send, r_recv,
):
    n_span, n_mp, rows, width, cols = sizes
    heads = cols // HD
    share = width // n_mp
    groups = kv.shape[2] // GROUP
    c = lax.axis_index("span")
    me = lax.axis_index("mp")
    phase = lax.axis_index("phase")
    is0 = phase == 0
    other = 1 - phase
    kept, sent = phase, 1 - phase
    sib = me + 1 - 2 * (me % 2)
    chips = n_mp // 2
    top = rows - MEM
    tail0 = HALF + top
    piece = MEM // CUTS
    last = n_span - 1

    def load(i, src, dst):
        copy = pltpu.make_async_copy(src, dst, load_sem.at[i])
        copy.start()
        return copy

    deep = width // 2
    rows_part = MEM // ROW_PARTS
    x_tails = []
    for n in range(ROW_PARTS):
        at = pl.ds(top + n * rows_part, rows_part)
        x_tails.append(load(n, x_hbm.at[at], x.at[at]))
        if n == 0:
            load(n, w_hbm.at[1 + sent, :, pl.ds(0, HD)], w.at[:, pl.ds(0, HD)])
    first_loads = w.at[:, pl.ds(0, rows_part + HD)]
    w_sent = load(ROW_PARTS, w_hbm.at[1 + sent, :, pl.ds(HD, cols - HD)], w.at[:, pl.ds(HD, cols - HD)])
    w_kept = load(ROW_PARTS + 1, w_hbm.at[1 + kept], w.at[:, pl.ds(cols, cols)])
    w_query = load(ROW_PARTS + 2, w_hbm.at[0], w.at[:, pl.ds(2 * cols, cols)])
    small = [
        load(ROW_PARTS + 3, decay_hbm, decay), load(ROW_PARTS + 4, frames_hbm, frames), load(ROW_PARTS + 5, opened_hbm, opened),
    ]
    x_head = load(ROW_PARTS + 6, x_hbm.at[pl.ds(0, top)], x.at[pl.ds(0, top)])
    wo_own = load(ROW_PARTS + 7, wo_hbm.at[:, pl.ds(pl.multiple_of(me * share, HD), share)], wo.at[me])

    barrier = pltpu.get_barrier_semaphore()
    for o in range(1, n_mp):
        pl.semaphore_signal(barrier, inc=1, device_id={"mp": (me + o) % n_mp}, device_id_type=MESH)
    pl.semaphore_signal(barrier, inc=1, device_id={"phase": other}, device_id_type=MESH)

    @pl.when(c > 0)
    def _():
        pl.semaphore_signal(barrier, inc=1, device_id={"span": c - 1}, device_id_type=MESH)

    @pl.when(c < last)
    def _():
        pl.semaphore_signal(barrier, inc=1, device_id={"span": c + 1}, device_id_type=MESH)

    zero_rows = kv.shape[2] - (HALF + rows + HALF)
    kv[:, :, HALF + rows + HALF:, :] = jnp.zeros((2, heads, zero_rows, HD), jnp.bfloat16)
    q[:, HALF + rows:, :] = jnp.zeros((heads, q.shape[1] - HALF - rows, HD), jnp.bfloat16)
    q[:, :HALF, :] = jnp.zeros((heads, HALF, HD), jnp.bfloat16)
    blank = pl.multiple_of(phase * (HALF + rows), HALF)
    kv[:, :, pl.ds(blank, HALF), :] = jnp.zeros((2, heads, HALF, HD), jnp.bfloat16)

    @pl.when(c == 0)
    def _():
        s_in[...] = jnp.zeros(s_in.shape, s_in.dtype)

    block = HD // 2
    parity = (c + phase) % 2

    def columns_of(m):
        return pl.ds(pl.multiple_of(m * share, HD), share)

    wo_copies, wo_downs, wo_ups, wo_acrosses, far = [], [], {}, [], []
    acrosses = range(chips - 1, 2 * (chips - 1))
    for o in range(1, chips):
        for near in (me, sib):
            far.append((near + n_mp - 2 * o) % n_mp)
    for i in range(heads):
        part = pl.ds(pl.multiple_of(i * HD + parity * block, block), block)
        for o in range(1, chips):
            for near in (me, sib):
                to, source = (near + 2 * o) % n_mp, (near + n_mp - 2 * o) % n_mp
                at = len(wo_copies)
                wo_copies.append(remote(
                    wo_hbm.at[part, columns_of(to)], wo.at[me, part],
                    wo_send, wo_recv.at[at], {"mp": to},
                ))
                held = wo.at[source, part]
                wo_downs.append(remote(held, held, wd_send, wr_recv.at[i], {"span": (c + last) % n_span}))
                if at in acrosses:
                    wo_acrosses.append(remote(held, held, wu_send, wr_recv.at[i], {"phase": other}))
                else:
                    wo_ups[at] = remote(held, held, wu_send, wr_recv.at[i], {"span": (c + 1) % n_span})
    wo_side = remote(wo_hbm.at[:, columns_of(sib)], wo.at[me], ws_send, ws_recv, {"mp": sib})
    per_head = len(far)

    lazy = (c == 0) & (n_span > 2)

    def relay(at):
        @pl.when(jnp.logical_not(lazy))
        def _():
            with scope("relay"):
                wo_copies[at].wait_recv()

        @pl.when(c > 0)
        def _():
            wo_downs[at].start()

    def relay_up(first, end):
        @pl.when(c == last - 1)
        def _():
            for at in range(first, end):
                wo_ups[at].start()

    def unit(part, flag):
        scale = lax.rsqrt(jnp.mean(part * part, axis=-1, keepdims=True) + epsilon)
        if flag is not None:
            scale = jnp.where(flag, scale, 1.0)
        return (part * scale).astype(jnp.bfloat16)

    def project(first, count, column, size):
        return jnp.dot(
            x[first:first + count, :], w[:, column:column + size],
            preferred_element_type=jnp.float32,
        )

    def tail_copy(k, i, r):
        return remote(
            kv.at[sent, i, pl.ds(tail0 + r * piece, piece)], tail_in.at[i, pl.ds(r * piece, piece)],
            y_send, y_recv.at[k], {"phase": other},
        )

    def chain_copy(k, i, r):
        at = pl.ds(r * piece, piece)
        return remote(s_out.at[i, at], s_in.at[i, at], z_send, z_recv.at[k], {"span": (c + 1) % n_span})

    def moved_copy(k, i, r):
        at = pl.ds(r * piece, piece)
        return remote(m_out.at[i, at], mem.at[kept, i, at], m_send, m_recv.at[i], {"phase": other})

    def each(make):
        return [make(i * CUTS + r, i, r) for i in range(heads) for r in range(CUTS)]

    tails = each(tail_copy)

    def keep(raw, first, count, n, at):
        part = raw[:, at * HD:(at + 1) * HD]
        rows_at = slice(HALF + first, HALF + first + count)
        if n >= 2 * heads:
            q[n - 2 * heads, rows_at, :] = unit(part, None)
        else:
            which = sent if n < heads else kept
            kv[which, n % heads, rows_at, :] = unit(part, which == 0)

    def columns(first, count, n, end):
        raw = project(first, count, n * HD, (end - n) * HD)
        for at in range(end - n):
            keep(raw, first, count, n + at, at)

    def send_tail(i):
        for r in range(CUTS):
            tails[i * CUTS + r].start()

    begun = 0

    def send_columns(count):
        nonlocal begun
        for copy in wo_copies[begun:begun + count]:
            copy.start()
        begun += count

    for n in range(ROW_PARTS):
        with scope("load%d" % n):
            if n == 0:
                pltpu.make_async_copy(first_loads, first_loads, load_sem.at[n]).wait()
            else:
                x_tails[n].wait()
        first = top + n * rows_part
        with scope("sent%d" % n):
            raw = jnp.dot(
                x[first:first + rows_part, :deep], w[:deep, :HD], preferred_element_type=jnp.float32
            ) + jnp.dot(
                x[first:first + rows_part, deep:], w[deep:, :HD], preferred_element_type=jnp.float32
            )
            keep(raw, first, rows_part, 0, 0)
        if n == 0:
            with scope("bar"):
                pl.semaphore_wait(barrier, n_mp + 1 + (c + n_span - 1) // n_span - (c + 1) // n_span)
        for r in range(n * CUTS // ROW_PARTS, (n + 1) * CUTS // ROW_PARTS):
            tails[r].start()
        if n == 0:
            send_columns(2 * (chips - 1))
    wo_side.start()
    for copy in small:
        copy.wait()
    wide = -(-(3 * heads - 1) // 2)
    with scope("loadk"):
        w_sent.wait()
        w_kept.wait()
    with scope("tail1"):
        columns(top, MEM, 1, 1 + wide)
    send_tail(1)
    send_columns(chips - 1)
    with scope("loadq"):
        w_query.wait()
    with scope("tail2"):
        columns(top, MEM, 1 + wide, 3 * heads)
    for i in range(2, heads):
        send_tail(i)
    with scope("loadx"):
        x_head.wait()
    halo_from = pl.multiple_of(HALF + other * (rows - HALF), HALF)
    halo = remote(
        kv.at[:, :, pl.ds(halo_from, HALF)], kv.at[:, :, pl.ds(blank, HALF)],
        h_send, h_recv, {"phase": other},
    )

    def rate_of(half, i):
        rate = decay[half:half + 1, 0:1]
        for n in range(1, heads):
            rate = jnp.where(i == n, decay[half:half + 1, n:n + 1], rate)
        return jnp.broadcast_to(rate, (1, HD))

    def mix(rate):
        return jnp.where(is0, 1.0 - rate, jnp.sqrt(1.0 - rate * rate))

    def chain_head(i):
        r0, r1 = rate_of(0, i), rate_of(1, i)
        f0, f1, both = mix(r0), mix(r1), r0 * r1
        for r in range(CUTS):
            k = i * CUTS + r
            rows_at = pl.ds(r * piece, piece)
            own = kv[kept, i, tail0 + r * piece:tail0 + (r + 1) * piece, :].astype(jnp.float32)
            with scope("waittail"):
                tail_copy(k, i, r).wait_recv()
            theirs = tail_in[i, rows_at, :].astype(jnp.float32)
            low = f0 * jnp.where(is0, own, theirs)
            high = r1 * low + f1 * jnp.where(is0, theirs, own)

            @pl.when(c > 0)
            def _():
                with scope("waitchain"):
                    chain_copy(k, i, r).wait_recv()

            state = s_in[i, rows_at, :].astype(jnp.float32)
            s_out[i, rows_at, :] = (both * state + high).astype(jnp.bfloat16)

            @pl.when(c < last)
            def _():
                chain_copy(k, i, r).start()

            later = r0 * state + low
            m_out[i, rows_at, :] = jnp.where(is0, later, state).astype(jnp.bfloat16)

            @pl.when(c > 0)
            def _():
                moved_copy(k, i, r).start()

            mem[kept, i, rows_at, :] = jnp.where(is0, state, later).astype(jnp.bfloat16)

    def frame_rows():
        total = frames.shape[1]
        wide = jnp.broadcast_to(frames[...], (8, total))
        ahead = pltpu.roll(wide, HALF, 1)
        behind = pltpu.roll(wide, total - (rows - HALF), 1)
        place = lax.broadcasted_iota(jnp.int32, wide.shape, 1)
        ext = jnp.where(is0, ahead, behind)
        least = jnp.where(is0, HALF, 0)
        limit = jnp.where(is0, total + HALF, rows + HALF)
        ext = jnp.where((place >= least) & (place < limit), ext, outside_frame)
        for g in range(groups):
            fr[g] = ext[:, g * GROUP:(g + 1) * GROUP].astype(jnp.float32)

    def local_group(g):
        at = pl.ds(g * GROUP, GROUP)
        key_frame = jnp.broadcast_to(fr[g][0:1, :], (GROUP, GROUP))
        same = (
            lax.broadcasted_iota(jnp.int32, (GROUP, GROUP), 0) // WIN
            == lax.broadcasted_iota(jnp.int32, (GROUP, GROUP), 1) // WIN
        )
        allowed = same & (key_frame <= key_frame.T)
        scores = [
            lax.dot_general(
                q[i, at, :], kv[0, i, at, :],
                (((1,), (1,)), ((), ())), preferred_element_type=jnp.float32,
            )
            for i in range(heads)
        ]
        weights = [jnp.where(allowed, jnp.exp2(score * score_factor), 0.0) for score in scores]
        values = [
            jnp.dot(weights[i].astype(jnp.bfloat16), kv[1, i, at, :], preferred_element_type=jnp.float32)
            for i in range(heads)
        ]
        for i in range(heads):
            den[i, at, :] = weights[i]
            num[i, at, :] = values[i]

    spots = [(i, n * 2 * GROUP, 2 * GROUP) for i in range(heads - 1) for n in range(rows // (2 * GROUP))]
    spots += [(heads - 1, n * GROUP, GROUP) for n in range(rows // GROUP)]
    sides, crosses, relays = [], [], []
    for j, (i, first, count) in enumerate(spots):
        at = pl.ds(first, count)
        mine = att.at[me, i, at]
        sides.append(remote(mine, mine, a_send, a_recv, {"mp": sib}))
        across, passed = [], []
        for o in range(1, chips):
            to = (me + 2 * o) % n_mp
            theirs = att.at[(me + n_mp - 2 * o) % n_mp, i, at]
            across.append(remote(mine, mine, c_send, c_recv.at[j, o - 1], {"mp": to}))
            passed.append(remote(theirs, theirs, r_send, r_recv.at[max(j - len(spots) + rows // GROUP + 1, 0)], {"mp": sib}))
        crosses.append(across)
        relays.append(passed)

    direct = {}
    for n, j in enumerate(range(len(spots) - DIRECT, len(spots))):
        i, first, count = spots[j]
        mine = att.at[me, i, pl.ds(first, count)]
        direct[j] = [
            remote(mine, mine, r_send, r_recv.at[1 + rows // GROUP - DIRECT + n], {"mp": (sib + 2 * o) % n_mp})
            for o in range(1, chips)
        ]
    even = me % 2 == 0

    start = phase * (rows // WIN)

    def memory_groups(i, members):
        scores, flagged = [], []
        for g in members:
            window = start + g * (GROUP // WIN)
            row = lax.broadcasted_iota(jnp.int32, (GROUP, MEM), 0)
            flags = opened[0, window + GROUP // WIN]
            for n in range(GROUP // WIN - 1, -1, -1):
                flags = jnp.where(row < HALF + n * WIN, opened[0, window + n], flags)
            flagged.append(flags == 1)
            scores.append(lax.dot_general(
                q[i, HALF + g * GROUP:HALF + (g + 1) * GROUP, :], mem[0, i],
                (((1,), (1,)), ((), ())), preferred_element_type=jnp.float32,
            ))
        weights = [
            jnp.where(flags, jnp.exp2(score * score_factor), 0.0) for score, flags in zip(scores, flagged)
        ]
        values = [
            jnp.dot(weight.astype(jnp.bfloat16), mem[1, i], preferred_element_type=jnp.float32)
            for weight in weights
        ]
        for g, weight, value in zip(members, weights, values):
            at = slice(HALF + g * GROUP, HALF + (g + 1) * GROUP)
            total = den[i, at, :]
            for j in range(MEM // HD):
                total = total + weight[:, j * HD:(j + 1) * HD]
            denom = jnp.sum(total, axis=-1, keepdims=True)
            att[me, i, g * GROUP:(g + 1) * GROUP, :] = ((num[i, at, :] + value) / denom).astype(jnp.bfloat16)

    def memory_head(i):
        with scope("waitmem"):
            remote(m_out.at[i], mem.at[kept, i], m_send, m_recv.at[i], {"phase": other}).wait_recv()
        with scope("mem"):
            for base in range(0, rows, 2 * GROUP):
                memory_groups(i, [base // GROUP, base // GROUP + 1])
                for j, (which, first, count) in enumerate(spots):
                    if which == i and base <= first < base + 2 * GROUP:
                        for copy in crosses[j]:
                            copy.start()
                        if j in direct:
                            @pl.when(even)
                            def _(copies=direct[j]):
                                for copy in copies:
                                    copy.start()
                        sides[j].start()

    def relay_head(i, n):
        for at in range(i * per_head + n * per_head // 2, i * per_head + (n + 1) * per_head // 2):
            relay(at)

    end = heads * per_head
    plan = {}
    for kind, spots_of in enumerate(PLAN):
        for i, place in enumerate(spots_of):
            plan.setdefault(place, []).append((kind, i))

    def chain_at(place):
        kind, i = jnp.minimum(c, len(PLAN) - 1), jnp.int32(heads)
        for which, head in plan[place]:
            if head < heads:
                i = jnp.where(kind == which, head, i)

        @pl.when(i < heads)
        def _():
            with scope("chain%d" % place):
                chain_head(i)

    chain_at(0)
    with scope("head1"):
        columns(0, top, 0, wide)
    send_columns(chips - 1)
    chain_at(1)

    @pl.when(c == 0)
    def _():
        for r in range(CUTS):
            moved_copy(r, 0, r).start()

    with scope("head2"):
        columns(0, top, wide, 2 * wide)
    halo.start()

    chain_at(2)

    @pl.when(c == 0)
    def _():
        for i in range(1, heads):
            for r in range(CUTS):
                moved_copy(i * CUTS + r, i, r).start()

    with scope("head3"):
        columns(0, top, 2 * wide, 3 * heads)
    send_columns(chips - 1)
    relay_head(0, 0)
    relay_up(0, acrosses[0])
    chain_at(3)
    with scope("local"):
        frame_rows()
        for g in range(1, groups - 1):
            local_group(g)
    send_columns(len(wo_copies))
    relay_head(0, 1)
    chain_at(4)
    with scope("local"):
        with scope("halo"):
            halo.wait_recv()
        local_group(0)
        local_group(groups - 1)
    relay_head(1, 0)
    chain_at(5)
    relay_head(1, 1)
    chain_at(6)
    memory_head(0)
    chain_at(7)
    relay_head(2, 0)
    memory_head(1)
    relay_head(2, 1)
    relay_up(per_head, heads * per_head)

    @pl.when(c == last)
    def _():
        for copy in wo_acrosses:
            copy.start()

    memory_head(2)

    own = pl.ds(pl.multiple_of(me * share, HD), share)

    def product(sources, which, first, count):
        left = jnp.concatenate([att[m, i, first:first + count, :] for m in sources for i in which], axis=1)
        right = jnp.concatenate([wo[m, i * HD:(i + 1) * HD, :] for m in sources for i in which], axis=0)
        return jnp.dot(left, right, preferred_element_type=jnp.float32)

    def add(sources, which, scope_name):
        with scope(scope_name):
            for first in range(0, rows, 2 * GROUP):
                at = slice(first, first + 2 * GROUP)
                acc[at, :] = acc[at, :] + product(sources, which, first, 2 * GROUP)

    def cross(j):
        for o in range(chips - 1):
            with scope("waitcross"):
                crosses[j][o].wait_recv()
            if j in direct:
                @pl.when(jnp.logical_not(even))
                def _(copy=relays[j][o]):
                    copy.start()
            else:
                relays[j][o].start()

    def arrived(lot, which):
        with scope("waitrelay"):
            remote(lot, lot, r_send, r_recv.at[which], {"mp": sib}).wait_recv()

    def far_weights(i):
        with scope("waitwo"):
            lot = wo.at[pl.ds(0, chips - 1), pl.ds(0, HD)]
            remote(lot, lot, wd_send, wr_recv.at[i], {"phase": other}).wait_recv()

            @pl.when(lazy)
            def _():
                for at in range(i * per_head, (i + 1) * per_head):
                    wo_copies[at].wait_recv()


    order = [[j for j, spot in enumerate(spots) if spot[0] == i] for i in range(heads)]
    wo_own.wait()
    with scope("own"):
        for first in range(0, rows, 2 * GROUP):
            at = slice(first, first + 2 * GROUP)
            acc[at, :] = x[at, own].astype(jnp.float32) + product([me], range(heads), first, 2 * GROUP)
    early = range(heads - 1)
    for j in order[0]:
        cross(j)
    with scope("waitside"):
        wo_side.wait_recv()
        remote(att.at[me], att.at[me], a_send, a_recv, {"mp": sib}).wait_recv()
    add([sib], range(heads), "near")
    for i in early[1:]:
        for j in order[i]:
            cross(j)
    for i in early:
        far_weights(i)
    add(far[0::2], early, "direct")
    final = order[heads - 1]
    half = len(final) // 2

    def passed():
        arrived(att.at[pl.ds(0, chips - 1), pl.ds(0, heads - 1)], 0)
        add(far[1::2], early, "passed")
        far_weights(heads - 1)

    def finish(n):
        first, count = spots[final[n]][1], half * spots[final[n]][2]
        for k in range(n, n + half):
            piece_at = pl.ds(spots[final[k]][1], spots[final[k]][2])
            arrived(att.at[pl.ds(0, chips - 1), heads - 1, piece_at], 1 + k)
        with scope("fin"):
            at = slice(first, first + count)
            out[at, :] = (acc[at, :] + product(far, [heads - 1], first, count)).astype(jnp.bfloat16)

    for j in final[:half]:
        cross(j)

    @pl.when(even)
    def _():
        passed()
        finish(0)

    for j in final[half:]:
        cross(j)

    @pl.when(jnp.logical_not(even))
    def _():
        passed()
        finish(0)

    finish(half)

    with scope("sends"):
        tail_all = kv.at[sent, :, pl.ds(tail0, MEM)]
        wo_all = wo.at[pl.ds(0, chips - 1)]
        att_all = att.at[pl.ds(0, chips - 1)]
        for src, send, recv, where in (
            (tail_all, y_send, y_recv.at[0], {"phase": other}),
            (m_out, m_send, m_recv.at[0], {"phase": other}),
            (wo_all, wo_send, wo_recv.at[0], {"mp": sib}),
            (att.at[me], a_send, a_recv, {"mp": sib}),
            (att_all, c_send, c_recv.at[0, 0], {"mp": sib}),
            (att_all, r_send, r_recv.at[0], {"mp": sib}),
        ):
            remote(src, src, send, recv, where).wait_send()
        halo.wait_send()
        wo_side.wait_send()

        @pl.when(c < last)
        def _():
            remote(s_out, s_in, z_send, z_recv.at[0], {"phase": other}).wait_send()

        @pl.when(c > 0)
        def _():
            remote(wo_all, wo_all, wd_send, wr_recv.at[0], {"phase": other}).wait_send()

        @pl.when(c == last - 1)
        def _():
            lot = wo.at[pl.ds(0, chips - 1), pl.ds(0, cols - block)]
            remote(lot, lot, wu_send, wr_recv.at[0], {"phase": other}).wait_send()

        @pl.when(c == last)
        def _():
            lot = wo.at[pl.ds(0, chips - 1), pl.ds(0, block)]
            remote(lot, lot, wu_send, wr_recv.at[0], {"phase": other}).wait_send()


def local(n_span, n_mp, latents, w_qkv, w_out, decay, frame_ids, memory_mask):
    rows, width = latents.shape
    cols = w_qkv.shape[2]
    heads = cols // HD
    share = width // n_mp
    ext = -(-(rows + WIN) // GROUP) * GROUP
    groups = ext // GROUP
    others = max(n_mp // 2 - 1, 1)
    chunks = 2 * others * heads
    pieces = heads * CUTS
    spots = (heads - 1) * (rows // (2 * GROUP)) + rows // GROUP
    hbm_spec = pl.BlockSpec(memory_space=pltpu.HBM)
    dma = pltpu.SemaphoreType.DMA
    bf16, f32 = jnp.bfloat16, jnp.float32
    flops = 2 * rows * width * 4 * cols
    inputs = (
        latents, jnp.transpose(w_qkv, (1, 0, 2)), w_out,
        decay.reshape(decay.shape[1:]), frame_ids, memory_mask,
    )
    return pl.pallas_call(
        functools.partial(body, (n_span, n_mp, rows, width, cols)),
        out_shape=jax.ShapeDtypeStruct((rows, share), bf16),
        in_specs=[hbm_spec] * 6,
        out_specs=pl.BlockSpec(memory_space=pltpu.VMEM),
        scratch_shapes=[
            pltpu.VMEM(decay.shape[1:], f32),
            pltpu.VMEM(frame_ids.shape, jnp.int32),
            pltpu.SMEM(memory_mask.shape, jnp.int32),
            pltpu.VMEM((rows, width), bf16),
            pltpu.VMEM((width, 3 * cols), bf16),
            pltpu.VMEM((n_mp, cols, share), bf16),
            pltpu.VMEM((2, heads, ext, HD), bf16),
            pltpu.VMEM((heads, ext, HD), bf16),
            pltpu.VMEM((heads, ext, HD), f32),
            pltpu.VMEM((heads, ext, HD), f32),
            pltpu.VMEM((n_mp, heads, rows, HD), bf16),
            pltpu.VMEM((rows, share), f32),
            pltpu.VMEM((groups, 8, GROUP), f32),
            pltpu.VMEM((heads, MEM, HD), bf16),
            pltpu.VMEM((heads, MEM, HD), bf16),
            pltpu.VMEM((heads, MEM, HD), bf16),
            pltpu.VMEM((heads, MEM, HD), bf16),
            pltpu.VMEM((2, heads, MEM, HD), bf16),
            dma((ROW_PARTS + 8,)),
            dma, dma,
            dma, dma((chunks,)), dma, dma, dma((heads,)),
            dma, dma((pieces,)),
            dma, dma((pieces,)),
            dma, dma((heads,)),
            dma, dma,
            dma, dma,
            dma, dma((spots, others)),
            dma, dma((1 + rows // GROUP,)),
        ],
        compiler_params=pltpu.CompilerParams(
            collective_id=0, has_side_effects=True, vmem_limit_bytes=40 * 1024 * 1024
        ),
        cost_estimate=pl.CostEstimate(flops=flops, bytes_accessed=12 << 20, transcendentals=1 << 20),
        name="refiner",
    )(*[pltpu.with_memory_space_constraint(a, pltpu.HBM) for a in inputs])


def solution(mesh):
    return jax.shard_map(
        functools.partial(local, mesh.shape["span"], mesh.shape["mp"]),
        mesh=mesh,
        in_specs=(
            P(("span", "phase"), None),
            P(None, None, "mp"),
            P("mp", None),
            P("span", None, "mp"),
            P("span", None),
            P("span", None),
        ),
        out_specs=P(("span", "phase"), "mp"),
        check_vma=False,
    )
```

```python
import contextlib
import functools
import math

import jax
import jax.numpy as jnp
from jax import lax
from jax.experimental import pallas as pl
from jax.experimental.pallas import tpu as pltpu
from jax.sharding import PartitionSpec as P

HD = 128
WIN = 64
MEM = 256
HALF = WIN // 2
GROUP = 128
CUTS = 4
DIRECT = 2
ROW_PARTS = 2
PLAN = ((0, 1, 2), (2, 3, 5), (4, 8, 7), (4, 6, 7))
MESH = pl.DeviceIdType.MESH

outside_frame = 1048576
epsilon = 1e-06
score_factor = HD ** (-0.5) * math.log2(math.e)


@contextlib.contextmanager
def scope(name):
    yield


def remote(src, dst, send, recv, where):
    return pltpu.make_async_remote_copy(
        src_ref=src, dst_ref=dst, send_sem=send, recv_sem=recv,
        device_id=where, device_id_type=MESH,
    )


def body(
    sizes, x_hbm, w_hbm, wo_hbm, decay_hbm, frames_hbm, opened_hbm, out,
    decay, frames, opened, x, w, wo, kv, q, num, den, att, acc, fr, tail_in, s_in, s_out, m_out, mem,
    load_sem, ws_send, ws_recv, wo_send, wo_recv, wd_send, wu_send, wr_recv, y_send, y_recv, z_send, z_recv, m_send, m_recv,
    h_send, h_recv, a_send, a_recv, c_send, c_recv, r_send, r_recv,
):
    n_span, n_mp, rows, width, cols = sizes
    heads = cols // HD
    share = width // n_mp
    groups = kv.shape[2] // GROUP
    c = lax.axis_index("span")
    me = lax.axis_index("mp")
    phase = lax.axis_index("phase")
    is0 = phase == 0
    other = 1 - phase
    kept, sent = phase, 1 - phase
    sib = me + 1 - 2 * (me % 2)
    chips = n_mp // 2
    top = rows - MEM
    tail0 = HALF + top
    piece = MEM // CUTS
    last = n_span - 1

    def load(i, src, dst):
        copy = pltpu.make_async_copy(src, dst, load_sem.at[i])
        copy.start()
        return copy

    deep = width // 2
    rows_part = MEM // ROW_PARTS
    x_tails = []
    for n in range(ROW_PARTS):
        at = pl.ds(top + n * rows_part, rows_part)
        x_tails.append(load(n, x_hbm.at[at], x.at[at]))
        if n == 0:
            load(n, w_hbm.at[1 + sent, :, pl.ds(0, HD)], w.at[:, pl.ds(0, HD)])
    first_loads = w.at[:, pl.ds(0, rows_part + HD)]
    load(ROW_PARTS, w_hbm.at[1 + sent, :, pl.ds(HD, cols - HD)], w.at[:, pl.ds(HD, cols - HD)])
    load(ROW_PARTS, w_hbm.at[1 + kept], w.at[:, pl.ds(cols, cols)])
    w_query = load(ROW_PARTS + 1, w_hbm.at[0], w.at[:, pl.ds(2 * cols, cols)])
    small = [
        load(ROW_PARTS + 2, decay_hbm, decay), load(ROW_PARTS + 3, frames_hbm, frames), load(ROW_PARTS + 4, opened_hbm, opened),
    ]
    x_head = load(ROW_PARTS + 5, x_hbm.at[pl.ds(0, top)], x.at[pl.ds(0, top)])
    wo_own = load(ROW_PARTS + 6, wo_hbm.at[:, pl.ds(pl.multiple_of(me * share, HD), share)], wo.at[me])

    barrier = pltpu.get_barrier_semaphore()
    for o in range(1, n_mp):
        pl.semaphore_signal(barrier, inc=1, device_id={"mp": (me + o) % n_mp}, device_id_type=MESH)
    pl.semaphore_signal(barrier, inc=1, device_id={"phase": other}, device_id_type=MESH)

    @pl.when(c > 0)
    def _():
        pl.semaphore_signal(barrier, inc=1, device_id={"span": c - 1}, device_id_type=MESH)

    @pl.when(c < last)
    def _():
        pl.semaphore_signal(barrier, inc=1, device_id={"span": c + 1}, device_id_type=MESH)

    zero_rows = kv.shape[2] - (HALF + rows + HALF)
    kv[:, :, HALF + rows + HALF:, :] = jnp.zeros((2, heads, zero_rows, HD), jnp.bfloat16)
    q[:, HALF + rows:, :] = jnp.zeros((heads, q.shape[1] - HALF - rows, HD), jnp.bfloat16)
    q[:, :HALF, :] = jnp.zeros((heads, HALF, HD), jnp.bfloat16)
    blank = pl.multiple_of(phase * (HALF + rows), HALF)
    kv[:, :, pl.ds(blank, HALF), :] = jnp.zeros((2, heads, HALF, HD), jnp.bfloat16)

    @pl.when(c == 0)
    def _():
        s_in[...] = jnp.zeros(s_in.shape, s_in.dtype)

    block = HD // 2
    parity = (c + phase) % 2

    def columns_of(m):
        return pl.ds(pl.multiple_of(m * share, HD), share)

    wo_copies, wo_downs, wo_ups, wo_acrosses, far = [], [], {}, [], []
    acrosses = range(chips - 1, 2 * (chips - 1))
    for o in range(1, chips):
        for near in (me, sib):
            far.append((near + n_mp - 2 * o) % n_mp)
    for i in range(heads):
        part = pl.ds(pl.multiple_of(i * HD + parity * block, block), block)
        for o in range(1, chips):
            for near in (me, sib):
                to, source = (near + 2 * o) % n_mp, (near + n_mp - 2 * o) % n_mp
                at = len(wo_copies)
                wo_copies.append(remote(
                    wo_hbm.at[part, columns_of(to)], wo.at[me, part],
                    wo_send, wo_recv.at[at], {"mp": to},
                ))
                held = wo.at[source, part]
                wo_downs.append(remote(held, held, wd_send, wr_recv.at[i], {"span": (c + last) % n_span}))
                if at in acrosses:
                    wo_acrosses.append(remote(held, held, wu_send, wr_recv.at[i], {"phase": other}))
                else:
                    wo_ups[at] = remote(held, held, wu_send, wr_recv.at[i], {"span": (c + 1) % n_span})
    wo_side = remote(wo_hbm.at[:, columns_of(sib)], wo.at[me], ws_send, ws_recv, {"mp": sib})
    per_head = len(far)

    lazy = (c == 0) & (n_span > 2)

    def relay(at):
        @pl.when(jnp.logical_not(lazy))
        def _():
            with scope("relay"):
                wo_copies[at].wait_recv()

        @pl.when(c > 0)
        def _():
            wo_downs[at].start()

    def relay_up(first, end):
        @pl.when(c == last - 1)
        def _():
            for at in range(first, end):
                wo_ups[at].start()

    def unit(part, flag):
        scale = lax.rsqrt(jnp.mean(part * part, axis=-1, keepdims=True) + epsilon)
        if flag is not None:
            scale = jnp.where(flag, scale, 1.0)
        return (part * scale).astype(jnp.bfloat16)

    def project(first, count, column, size):
        return jnp.dot(
            x[first:first + count, :], w[:, column:column + size],
            preferred_element_type=jnp.float32,
        )

    def tail_copy(k, i, r):
        return remote(
            kv.at[sent, i, pl.ds(tail0 + r * piece, piece)], tail_in.at[i, pl.ds(r * piece, piece)],
            y_send, y_recv.at[k], {"phase": other},
        )

    def chain_copy(k, i, r):
        at = pl.ds(r * piece, piece)
        return remote(s_out.at[i, at], s_in.at[i, at], z_send, z_recv.at[k], {"span": (c + 1) % n_span})

    def moved_copy(k, i, r):
        at = pl.ds(r * piece, piece)
        return remote(m_out.at[i, at], mem.at[kept, i, at], m_send, m_recv.at[i], {"phase": other})

    def each(make):
        return [make(i * CUTS + r, i, r) for i in range(heads) for r in range(CUTS)]

    tails = each(tail_copy)

    def keep(raw, first, count, n, at):
        part = raw[:, at * HD:(at + 1) * HD]
        rows_at = slice(HALF + first, HALF + first + count)
        if n >= 2 * heads:
            q[n - 2 * heads, rows_at, :] = unit(part, None)
        else:
            which = sent if n < heads else kept
            kv[which, n % heads, rows_at, :] = unit(part, which == 0)

    def columns(first, count, n, end):
        raw = project(first, count, n * HD, (end - n) * HD)
        for at in range(end - n):
            keep(raw, first, count, n + at, at)

    def send_tail(i):
        for r in range(CUTS):
            tails[i * CUTS + r].start()

    begun = 0

    def send_columns(count):
        nonlocal begun
        for copy in wo_copies[begun:begun + count]:
            copy.start()
        begun += count

    for n in range(ROW_PARTS):
        with scope("load%d" % n):
            if n == 0:
                pltpu.make_async_copy(first_loads, first_loads, load_sem.at[n]).wait()
            else:
                x_tails[n].wait()
        first = top + n * rows_part
        with scope("sent%d" % n):
            raw = jnp.dot(
                x[first:first + rows_part, :deep], w[:deep, :HD], preferred_element_type=jnp.float32
            ) + jnp.dot(
                x[first:first + rows_part, deep:], w[deep:, :HD], preferred_element_type=jnp.float32
            )
            keep(raw, first, rows_part, 0, 0)
        if n == 0:
            with scope("bar"):
                pl.semaphore_wait(barrier, n_mp + 1 + (c + n_span - 1) // n_span - (c + 1) // n_span)
        for r in range(n * CUTS // ROW_PARTS, (n + 1) * CUTS // ROW_PARTS):
            tails[r].start()
        if n == 0:
            send_columns(2 * (chips - 1))
    wo_side.start()
    for copy in small:
        copy.wait()
    wide = -(-(3 * heads - 1) // 2)
    with scope("loadk"):
        both = w.at[:, pl.ds(HD, 2 * cols - HD)]
        pltpu.make_async_copy(both, both, load_sem.at[ROW_PARTS]).wait()
    with scope("tail1"):
        columns(top, MEM, 1, 1 + wide)
    send_tail(1)
    send_columns(chips - 1)
    with scope("loadq"):
        w_query.wait()
    with scope("tail2"):
        columns(top, MEM, 1 + wide, 3 * heads)
    for i in range(2, heads):
        send_tail(i)
    with scope("loadx"):
        x_head.wait()
    halo_from = pl.multiple_of(HALF + other * (rows - HALF), HALF)
    halo = remote(
        kv.at[:, :, pl.ds(halo_from, HALF)], kv.at[:, :, pl.ds(blank, HALF)],
        h_send, h_recv, {"phase": other},
    )

    def rate_of(half, i):
        rate = decay[half:half + 1, 0:1]
        for n in range(1, heads):
            rate = jnp.where(i == n, decay[half:half + 1, n:n + 1], rate)
        return jnp.broadcast_to(rate, (1, HD))

    def mix(rate):
        return jnp.where(is0, 1.0 - rate, jnp.sqrt(1.0 - rate * rate))

    def chain_head(i):
        r0, r1 = rate_of(0, i), rate_of(1, i)
        f0, f1, both = mix(r0), mix(r1), r0 * r1
        for r in range(CUTS):
            k = i * CUTS + r
            rows_at = pl.ds(r * piece, piece)
            own = kv[kept, i, tail0 + r * piece:tail0 + (r + 1) * piece, :].astype(jnp.float32)
            with scope("waittail"):
                tail_copy(k, i, r).wait_recv()
            theirs = tail_in[i, rows_at, :].astype(jnp.float32)
            low = f0 * jnp.where(is0, own, theirs)
            high = r1 * low + f1 * jnp.where(is0, theirs, own)

            @pl.when(c > 0)
            def _():
                with scope("waitchain"):
                    chain_copy(k, i, r).wait_recv()

            state = s_in[i, rows_at, :].astype(jnp.float32)
            s_out[i, rows_at, :] = (both * state + high).astype(jnp.bfloat16)

            @pl.when(c < last)
            def _():
                chain_copy(k, i, r).start()

            later = r0 * state + low
            m_out[i, rows_at, :] = jnp.where(is0, later, state).astype(jnp.bfloat16)

            @pl.when(c > 0)
            def _():
                moved_copy(k, i, r).start()

            mem[kept, i, rows_at, :] = jnp.where(is0, state, later).astype(jnp.bfloat16)

    def frame_rows():
        total = frames.shape[1]
        wide = jnp.broadcast_to(frames[...], (8, total))
        ahead = pltpu.roll(wide, HALF, 1)
        behind = pltpu.roll(wide, total - (rows - HALF), 1)
        place = lax.broadcasted_iota(jnp.int32, wide.shape, 1)
        ext = jnp.where(is0, ahead, behind)
        least = jnp.where(is0, HALF, 0)
        limit = jnp.where(is0, total + HALF, rows + HALF)
        ext = jnp.where((place >= least) & (place < limit), ext, outside_frame)
        for g in range(groups):
            fr[g] = ext[:, g * GROUP:(g + 1) * GROUP].astype(jnp.float32)

    def local_group(g):
        at = pl.ds(g * GROUP, GROUP)
        key_frame = jnp.broadcast_to(fr[g][0:1, :], (GROUP, GROUP))
        same = (
            lax.broadcasted_iota(jnp.int32, (GROUP, GROUP), 0) // WIN
            == lax.broadcasted_iota(jnp.int32, (GROUP, GROUP), 1) // WIN
        )
        allowed = same & (key_frame <= key_frame.T)
        scores = [
            lax.dot_general(
                q[i, at, :], kv[0, i, at, :],
                (((1,), (1,)), ((), ())), preferred_element_type=jnp.float32,
            )
            for i in range(heads)
        ]
        weights = [jnp.where(allowed, jnp.exp2(score * score_factor), 0.0) for score in scores]
        values = [
            jnp.dot(weights[i].astype(jnp.bfloat16), kv[1, i, at, :], preferred_element_type=jnp.float32)
            for i in range(heads)
        ]
        for i in range(heads):
            den[i, at, :] = weights[i]
            num[i, at, :] = values[i]

    spots = [(i, n * 2 * GROUP, 2 * GROUP) for i in range(heads - 1) for n in range(rows // (2 * GROUP))]
    spots += [(heads - 1, n * GROUP, GROUP) for n in range(rows // GROUP)]
    sides, crosses, relays = [], [], []
    for j, (i, first, count) in enumerate(spots):
        at = pl.ds(first, count)
        mine = att.at[me, i, at]
        sides.append(remote(mine, mine, a_send, a_recv, {"mp": sib}))
        across, passed = [], []
        for o in range(1, chips):
            to = (me + 2 * o) % n_mp
            theirs = att.at[(me + n_mp - 2 * o) % n_mp, i, at]
            across.append(remote(mine, mine, c_send, c_recv.at[j, o - 1], {"mp": to}))
            passed.append(remote(theirs, theirs, r_send, r_recv.at[max(j - len(spots) + rows // GROUP + 1, 0)], {"mp": sib}))
        crosses.append(across)
        relays.append(passed)

    direct = {}
    for n, j in enumerate(range(len(spots) - DIRECT, len(spots))):
        i, first, count = spots[j]
        mine = att.at[me, i, pl.ds(first, count)]
        direct[j] = [
            remote(mine, mine, r_send, r_recv.at[1 + rows // GROUP - DIRECT + n], {"mp": (sib + 2 * o) % n_mp})
            for o in range(1, chips)
        ]
    even = me % 2 == 0

    start = phase * (rows // WIN)

    def memory_groups(i, members):
        scores, flagged = [], []
        for g in members:
            window = start + g * (GROUP // WIN)
            row = lax.broadcasted_iota(jnp.int32, (GROUP, MEM), 0)
            flags = opened[0, window + GROUP // WIN]
            for n in range(GROUP // WIN - 1, -1, -1):
                flags = jnp.where(row < HALF + n * WIN, opened[0, window + n], flags)
            flagged.append(flags == 1)
            scores.append(lax.dot_general(
                q[i, HALF + g * GROUP:HALF + (g + 1) * GROUP, :], mem[0, i],
                (((1,), (1,)), ((), ())), preferred_element_type=jnp.float32,
            ))
        weights = [
            jnp.where(flags, jnp.exp2(score * score_factor), 0.0) for score, flags in zip(scores, flagged)
        ]
        values = [
            jnp.dot(weight.astype(jnp.bfloat16), mem[1, i], preferred_element_type=jnp.float32)
            for weight in weights
        ]
        for g, weight, value in zip(members, weights, values):
            at = slice(HALF + g * GROUP, HALF + (g + 1) * GROUP)
            total = den[i, at, :]
            for j in range(MEM // HD):
                total = total + weight[:, j * HD:(j + 1) * HD]
            denom = jnp.sum(total, axis=-1, keepdims=True)
            att[me, i, g * GROUP:(g + 1) * GROUP, :] = ((num[i, at, :] + value) / denom).astype(jnp.bfloat16)

    def memory_head(i):
        with scope("waitmem"):
            remote(m_out.at[i], mem.at[kept, i], m_send, m_recv.at[i], {"phase": other}).wait_recv()
        with scope("mem"):
            for base in range(0, rows, 2 * GROUP):
                memory_groups(i, [base // GROUP, base // GROUP + 1])
                for j, (which, first, count) in enumerate(spots):
                    if which == i and base <= first < base + 2 * GROUP:
                        for copy in crosses[j]:
                            copy.start()
                        if j in direct:
                            @pl.when(even)
                            def _(copies=direct[j]):
                                for copy in copies:
                                    copy.start()
                        sides[j].start()

    def relay_head(i, n):
        for at in range(i * per_head + n * per_head // 2, i * per_head + (n + 1) * per_head // 2):
            relay(at)

    end = heads * per_head
    plan = {}
    for kind, spots_of in enumerate(PLAN):
        for i, place in enumerate(spots_of):
            plan.setdefault(place, []).append((kind, i))

    def chain_at(place):
        kind, i = jnp.minimum(c, len(PLAN) - 1), jnp.int32(heads)
        for which, head in plan[place]:
            if head < heads:
                i = jnp.where(kind == which, head, i)

        @pl.when(i < heads)
        def _():
            with scope("chain%d" % place):
                chain_head(i)

    chain_at(0)
    with scope("head1"):
        columns(0, top, 0, wide)
    send_columns(len(wo_copies))
    chain_at(1)

    @pl.when(c == 0)
    def _():
        for r in range(CUTS):
            moved_copy(r, 0, r).start()

    with scope("head2"):
        columns(0, top, wide, 2 * wide)
    halo.start()

    chain_at(2)

    @pl.when(c == 0)
    def _():
        for i in range(1, heads):
            for r in range(CUTS):
                moved_copy(i * CUTS + r, i, r).start()

    with scope("head3"):
        columns(0, top, 2 * wide, 3 * heads)
    relay_head(0, 0)
    relay_up(0, acrosses[0])
    chain_at(3)
    with scope("local"):
        frame_rows()
        for g in range(1, groups - 1):
            local_group(g)
    relay_head(0, 1)
    chain_at(4)
    chain_at(8)
    with scope("local"):
        with scope("halo"):
            halo.wait_recv()
        local_group(0)
        local_group(groups - 1)
    relay_head(1, 0)
    chain_at(5)
    relay_head(1, 1)
    chain_at(6)
    memory_head(0)
    chain_at(7)
    relay_head(2, 0)
    memory_head(1)
    relay_head(2, 1)
    relay_up(per_head, heads * per_head)

    @pl.when(c == last)
    def _():
        for copy in wo_acrosses:
            copy.start()

    memory_head(2)

    own = pl.ds(pl.multiple_of(me * share, HD), share)

    def product(sources, which, first, count):
        left = jnp.concatenate([att[m, i, first:first + count, :] for m in sources for i in which], axis=1)
        right = jnp.concatenate([wo[m, i * HD:(i + 1) * HD, :] for m in sources for i in which], axis=0)
        return jnp.dot(left, right, preferred_element_type=jnp.float32)

    def add(sources, which, scope_name):
        with scope(scope_name):
            for first in range(0, rows, 2 * GROUP):
                at = slice(first, first + 2 * GROUP)
                acc[at, :] = acc[at, :] + product(sources, which, first, 2 * GROUP)

    def cross(j):
        for o in range(chips - 1):
            with scope("waitcross"):
                crosses[j][o].wait_recv()
            if j in direct:
                @pl.when(jnp.logical_not(even))
                def _(copy=relays[j][o]):
                    copy.start()
            else:
                relays[j][o].start()

    def arrived(lot, which):
        with scope("waitrelay"):
            remote(lot, lot, r_send, r_recv.at[which], {"mp": sib}).wait_recv()

    def far_weights(i):
        with scope("waitwo"):
            lot = wo.at[pl.ds(0, chips - 1), pl.ds(0, HD)]
            remote(lot, lot, wd_send, wr_recv.at[i], {"phase": other}).wait_recv()

            @pl.when(lazy)
            def _():
                for at in range(i * per_head, (i + 1) * per_head):
                    wo_copies[at].wait_recv()


    order = [[j for j, spot in enumerate(spots) if spot[0] == i] for i in range(heads)]
    wo_own.wait()
    with scope("own"):
        for first in range(0, rows, 2 * GROUP):
            at = slice(first, first + 2 * GROUP)
            acc[at, :] = x[at, own].astype(jnp.float32) + product([me], range(heads), first, 2 * GROUP)
    early = range(heads - 1)
    for j in order[0]:
        cross(j)
    with scope("waitside"):
        wo_side.wait_recv()
        remote(att.at[me], att.at[me], a_send, a_recv, {"mp": sib}).wait_recv()
    add([sib], range(heads), "near")
    for i in early[1:]:
        for j in order[i]:
            cross(j)
    for i in early:
        far_weights(i)
    add(far[0::2], early, "direct")
    final = order[heads - 1]
    half = len(final) // 2

    def passed():
        arrived(att.at[pl.ds(0, chips - 1), pl.ds(0, heads - 1)], 0)
        add(far[1::2], early, "passed")
        far_weights(heads - 1)

    def finish(n, size):
        first, count = spots[final[n]][1], size * spots[final[n]][2]
        for k in range(n, n + size):
            piece_at = pl.ds(spots[final[k]][1], spots[final[k]][2])
            arrived(att.at[pl.ds(0, chips - 1), heads - 1, piece_at], 1 + k)
        with scope("fin"):
            at = slice(first, first + count)
            out[at, :] = (acc[at, :] + product(far, [heads - 1], first, count)).astype(jnp.bfloat16)

    for j in final[:half]:
        cross(j)

    @pl.when(even)
    def _():
        passed()
        finish(0, half)

    for j in final[half:]:
        cross(j)

    @pl.when(even)
    def _():
        finish(half, len(final) - half)

    @pl.when(jnp.logical_not(even))
    def _():
        passed()
        finish(0, len(final))

    with scope("sends"):
        tail_all = kv.at[sent, :, pl.ds(tail0, MEM)]
        wo_all = wo.at[pl.ds(0, chips - 1)]
        att_all = att.at[pl.ds(0, chips - 1)]
        for src, send, recv, where in (
            (tail_all, y_send, y_recv.at[0], {"phase": other}),
            (m_out, m_send, m_recv.at[0], {"phase": other}),
            (wo_all, wo_send, wo_recv.at[0], {"mp": sib}),
            (att.at[me], a_send, a_recv, {"mp": sib}),
            (att_all, c_send, c_recv.at[0, 0], {"mp": sib}),
            (att_all, r_send, r_recv.at[0], {"mp": sib}),
        ):
            remote(src, src, send, recv, where).wait_send()
        halo.wait_send()
        wo_side.wait_send()

        @pl.when(c < last)
        def _():
            remote(s_out, s_in, z_send, z_recv.at[0], {"phase": other}).wait_send()

        @pl.when(c > 0)
        def _():
            remote(wo_all, wo_all, wd_send, wr_recv.at[0], {"phase": other}).wait_send()

        @pl.when(c == last - 1)
        def _():
            lot = wo.at[pl.ds(0, chips - 1), pl.ds(0, cols - block)]
            remote(lot, lot, wu_send, wr_recv.at[0], {"phase": other}).wait_send()

        @pl.when(c == last)
        def _():
            lot = wo.at[pl.ds(0, chips - 1), pl.ds(0, block)]
            remote(lot, lot, wu_send, wr_recv.at[0], {"phase": other}).wait_send()


def local(n_span, n_mp, latents, w_qkv, w_out, decay, frame_ids, memory_mask):
    rows, width = latents.shape
    cols = w_qkv.shape[2]
    heads = cols // HD
    share = width // n_mp
    ext = -(-(rows + WIN) // GROUP) * GROUP
    groups = ext // GROUP
    others = max(n_mp // 2 - 1, 1)
    chunks = 2 * others * heads
    pieces = heads * CUTS
    spots = (heads - 1) * (rows // (2 * GROUP)) + rows // GROUP
    hbm_spec = pl.BlockSpec(memory_space=pltpu.HBM)
    dma = pltpu.SemaphoreType.DMA
    bf16, f32 = jnp.bfloat16, jnp.float32
    flops = 2 * rows * width * 4 * cols
    inputs = (
        latents, jnp.transpose(w_qkv, (1, 0, 2)), w_out,
        decay.reshape(decay.shape[1:]), frame_ids, memory_mask,
    )
    return pl.pallas_call(
        functools.partial(body, (n_span, n_mp, rows, width, cols)),
        out_shape=jax.ShapeDtypeStruct((rows, share), bf16),
        in_specs=[hbm_spec] * 6,
        out_specs=pl.BlockSpec(memory_space=pltpu.VMEM),
        scratch_shapes=[
            pltpu.VMEM(decay.shape[1:], f32),
            pltpu.VMEM(frame_ids.shape, jnp.int32),
            pltpu.SMEM(memory_mask.shape, jnp.int32),
            pltpu.VMEM((rows, width), bf16),
            pltpu.VMEM((width, 3 * cols), bf16),
            pltpu.VMEM((n_mp, cols, share), bf16),
            pltpu.VMEM((2, heads, ext, HD), bf16),
            pltpu.VMEM((heads, ext, HD), bf16),
            pltpu.VMEM((heads, ext, HD), f32),
            pltpu.VMEM((heads, ext, HD), f32),
            pltpu.VMEM((n_mp, heads, rows, HD), bf16),
            pltpu.VMEM((rows, share), f32),
            pltpu.VMEM((groups, 8, GROUP), f32),
            pltpu.VMEM((heads, MEM, HD), bf16),
            pltpu.VMEM((heads, MEM, HD), bf16),
            pltpu.VMEM((heads, MEM, HD), bf16),
            pltpu.VMEM((heads, MEM, HD), bf16),
            pltpu.VMEM((2, heads, MEM, HD), bf16),
            dma((ROW_PARTS + 7,)),
            dma, dma,
            dma, dma((chunks,)), dma, dma, dma((heads,)),
            dma, dma((pieces,)),
            dma, dma((pieces,)),
            dma, dma((heads,)),
            dma, dma,
            dma, dma,
            dma, dma((spots, others)),
            dma, dma((1 + rows // GROUP,)),
        ],
        compiler_params=pltpu.CompilerParams(
            collective_id=0, has_side_effects=True, vmem_limit_bytes=40 * 1024 * 1024
        ),
        cost_estimate=pl.CostEstimate(flops=flops, bytes_accessed=12 << 20, transcendentals=1 << 20),
        name="refiner",
    )(*[pltpu.with_memory_space_constraint(a, pltpu.HBM) for a in inputs])


def solution(mesh):
    return jax.shard_map(
        functools.partial(local, mesh.shape["span"], mesh.shape["mp"]),
        mesh=mesh,
        in_specs=(
            P(("span", "phase"), None),
            P(None, None, "mp"),
            P("mp", None),
            P("span", None, "mp"),
            P("span", None),
            P("span", None),
        ),
        out_specs=P(("span", "phase"), "mp"),
        check_vma=False,
    )
```

```python
import contextlib
import functools
import math

import jax
import jax.numpy as jnp
from jax import lax
from jax.experimental import pallas as pl
from jax.experimental.pallas import tpu as pltpu
from jax.sharding import PartitionSpec as P

HD = 128
WIN = 64
MEM = 256
HALF = WIN // 2
GROUP = 128
CUTS = 4
DIRECT = 2
ROW_PARTS = 2
PLAN = ((0, 1, 2), (2, 3, 4), (4, 8, 6), (4, 5, 7))
MESH = pl.DeviceIdType.MESH

outside_frame = 1048576
epsilon = 1e-06
score_factor = HD ** (-0.5) * math.log2(math.e)


@contextlib.contextmanager
def scope(name):
    yield


def remote(src, dst, send, recv, where):
    return pltpu.make_async_remote_copy(
        src_ref=src, dst_ref=dst, send_sem=send, recv_sem=recv,
        device_id=where, device_id_type=MESH,
    )


def body(
    sizes, x_hbm, w_hbm, wo_hbm, decay_hbm, frames_hbm, opened_hbm, out,
    decay, frames, opened, x, w, wo, kv, q, num, den, att, acc, fr, tail_in, s_in, s_out, m_out, mem,
    load_sem, ws_send, ws_recv, wo_send, wo_recv, wd_send, wu_send, wr_recv, y_send, y_recv, z_send, z_recv, m_send, m_recv,
    h_send, h_recv, a_send, a_recv, c_send, c_recv, r_send, r_recv,
):
    n_span, n_mp, rows, width, cols = sizes
    heads = cols // HD
    share = width // n_mp
    groups = kv.shape[2] // GROUP
    c = lax.axis_index("span")
    me = lax.axis_index("mp")
    phase = lax.axis_index("phase")
    is0 = phase == 0
    other = 1 - phase
    kept, sent = phase, 1 - phase
    sib = me + 1 - 2 * (me % 2)
    chips = n_mp // 2
    top = rows - MEM
    tail0 = HALF + top
    piece = MEM // CUTS
    last = n_span - 1

    def load(i, src, dst):
        copy = pltpu.make_async_copy(src, dst, load_sem.at[i])
        copy.start()
        return copy

    deep = width // 2
    rows_part = MEM // ROW_PARTS
    x_tails = []
    for n in range(ROW_PARTS):
        at = pl.ds(top + n * rows_part, rows_part)
        x_tails.append(load(n, x_hbm.at[at], x.at[at]))
        if n == 0:
            load(n, w_hbm.at[1 + sent, :, pl.ds(0, HD)], w.at[:, pl.ds(0, HD)])
    first_loads = w.at[:, pl.ds(0, rows_part + HD)]
    load(ROW_PARTS, w_hbm.at[1 + sent, :, pl.ds(HD, cols - HD)], w.at[:, pl.ds(HD, cols - HD)])
    load(ROW_PARTS, w_hbm.at[1 + kept], w.at[:, pl.ds(cols, cols)])
    w_query = load(ROW_PARTS + 1, w_hbm.at[0], w.at[:, pl.ds(2 * cols, cols)])
    small = [
        load(ROW_PARTS + 2, decay_hbm, decay), load(ROW_PARTS + 3, frames_hbm, frames), load(ROW_PARTS + 4, opened_hbm, opened),
    ]
    x_head = load(ROW_PARTS + 5, x_hbm.at[pl.ds(0, top)], x.at[pl.ds(0, top)])
    wo_own = load(ROW_PARTS + 6, wo_hbm.at[:, pl.ds(pl.multiple_of(me * share, HD), share)], wo.at[me])

    barrier = pltpu.get_barrier_semaphore()
    for o in range(1, n_mp):
        pl.semaphore_signal(barrier, inc=1, device_id={"mp": (me + o) % n_mp}, device_id_type=MESH)
    pl.semaphore_signal(barrier, inc=1, device_id={"phase": other}, device_id_type=MESH)

    @pl.when(c > 0)
    def _():
        pl.semaphore_signal(barrier, inc=1, device_id={"span": c - 1}, device_id_type=MESH)

    @pl.when(c < last)
    def _():
        pl.semaphore_signal(barrier, inc=1, device_id={"span": c + 1}, device_id_type=MESH)

    zero_rows = kv.shape[2] - (HALF + rows + HALF)
    kv[:, :, HALF + rows + HALF:, :] = jnp.zeros((2, heads, zero_rows, HD), jnp.bfloat16)
    q[:, HALF + rows:, :] = jnp.zeros((heads, q.shape[1] - HALF - rows, HD), jnp.bfloat16)
    q[:, :HALF, :] = jnp.zeros((heads, HALF, HD), jnp.bfloat16)
    blank = pl.multiple_of(phase * (HALF + rows), HALF)
    kv[:, :, pl.ds(blank, HALF), :] = jnp.zeros((2, heads, HALF, HD), jnp.bfloat16)

    @pl.when(c == 0)
    def _():
        s_in[...] = jnp.zeros(s_in.shape, s_in.dtype)

    block = HD // 2
    parity = (c + phase) % 2

    def columns_of(m):
        return pl.ds(pl.multiple_of(m * share, HD), share)

    wo_copies, wo_downs, wo_ups, wo_acrosses, far = [], [], {}, [], []
    acrosses = range(chips - 1, 2 * (chips - 1))
    for o in range(1, chips):
        for near in (me, sib):
            far.append((near + n_mp - 2 * o) % n_mp)
    for i in range(heads):
        part = pl.ds(pl.multiple_of(i * HD + parity * block, block), block)
        for o in range(1, chips):
            for near in (me, sib):
                to, source = (near + 2 * o) % n_mp, (near + n_mp - 2 * o) % n_mp
                at = len(wo_copies)
                wo_copies.append(remote(
                    wo_hbm.at[part, columns_of(to)], wo.at[me, part],
                    wo_send, wo_recv.at[at], {"mp": to},
                ))
                held = wo.at[source, part]
                wo_downs.append(remote(held, held, wd_send, wr_recv.at[i], {"span": (c + last) % n_span}))
                if at in acrosses:
                    wo_acrosses.append(remote(held, held, wu_send, wr_recv.at[i], {"phase": other}))
                else:
                    wo_ups[at] = remote(held, held, wu_send, wr_recv.at[i], {"span": (c + 1) % n_span})
    wo_side = remote(wo_hbm.at[:, columns_of(sib)], wo.at[me], ws_send, ws_recv, {"mp": sib})
    per_head = len(far)

    lazy = (c == 0) & (n_span > 2)

    def relay(at):
        @pl.when(jnp.logical_not(lazy))
        def _():
            with scope("relay"):
                wo_copies[at].wait_recv()

        @pl.when(c > 0)
        def _():
            wo_downs[at].start()

    def relay_up(first, end):
        @pl.when(c == last - 1)
        def _():
            for at in range(first, end):
                wo_ups[at].start()

    def unit(part, flag):
        scale = lax.rsqrt(jnp.mean(part * part, axis=-1, keepdims=True) + epsilon)
        if flag is not None:
            scale = jnp.where(flag, scale, 1.0)
        return (part * scale).astype(jnp.bfloat16)

    def project(first, count, column, size):
        return jnp.dot(
            x[first:first + count, :], w[:, column:column + size],
            preferred_element_type=jnp.float32,
        )

    def tail_copy(k, i, r):
        return remote(
            kv.at[sent, i, pl.ds(tail0 + r * piece, piece)], tail_in.at[i, pl.ds(r * piece, piece)],
            y_send, y_recv.at[k], {"phase": other},
        )

    def chain_copy(k, i, r):
        at = pl.ds(r * piece, piece)
        return remote(s_out.at[i, at], s_in.at[i, at], z_send, z_recv.at[k], {"span": (c + 1) % n_span})

    def moved_copy(k, i, r):
        at = pl.ds(r * piece, piece)
        return remote(m_out.at[i, at], mem.at[kept, i, at], m_send, m_recv.at[i], {"phase": other})

    def each(make):
        return [make(i * CUTS + r, i, r) for i in range(heads) for r in range(CUTS)]

    tails = each(tail_copy)

    def keep(raw, first, count, n, at):
        part = raw[:, at * HD:(at + 1) * HD]
        rows_at = slice(HALF + first, HALF + first + count)
        if n >= 2 * heads:
            q[n - 2 * heads, rows_at, :] = unit(part, None)
        else:
            which = sent if n < heads else kept
            kv[which, n % heads, rows_at, :] = unit(part, which == 0)

    def columns(first, count, n, end):
        raw = project(first, count, n * HD, (end - n) * HD)
        for at in range(end - n):
            keep(raw, first, count, n + at, at)

    def send_tail(i):
        for r in range(CUTS):
            tails[i * CUTS + r].start()

    begun = 0

    def send_columns(count):
        nonlocal begun
        for copy in wo_copies[begun:begun + count]:
            copy.start()
        begun += count

    for n in range(ROW_PARTS):
        with scope("load%d" % n):
            if n == 0:
                pltpu.make_async_copy(first_loads, first_loads, load_sem.at[n]).wait()
            else:
                x_tails[n].wait()
        first = top + n * rows_part
        with scope("sent%d" % n):
            raw = jnp.dot(
                x[first:first + rows_part, :deep], w[:deep, :HD], preferred_element_type=jnp.float32
            ) + jnp.dot(
                x[first:first + rows_part, deep:], w[deep:, :HD], preferred_element_type=jnp.float32
            )
            keep(raw, first, rows_part, 0, 0)
        if n == 0:
            with scope("bar"):
                pl.semaphore_wait(barrier, n_mp + 1 + (c + n_span - 1) // n_span - (c + 1) // n_span)
        for r in range(n * CUTS // ROW_PARTS, (n + 1) * CUTS // ROW_PARTS):
            tails[r].start()
        if n == 0:
            send_columns(2 * (chips - 1))
    wo_side.start()
    for copy in small:
        copy.wait()
    wide = -(-(3 * heads - 1) // 2)
    with scope("loadk"):
        both = w.at[:, pl.ds(HD, 2 * cols - HD)]
        pltpu.make_async_copy(both, both, load_sem.at[ROW_PARTS]).wait()
    with scope("tail1"):
        columns(top, MEM, 1, 1 + wide)
    send_tail(1)
    send_columns(chips - 1)
    with scope("loadq"):
        w_query.wait()
    with scope("tail2"):
        columns(top, MEM, 1 + wide, 3 * heads)
    for i in range(2, heads):
        send_tail(i)
    with scope("loadx"):
        x_head.wait()
    halo_from = pl.multiple_of(HALF + other * (rows - HALF), HALF)
    halo = remote(
        kv.at[:, :, pl.ds(halo_from, HALF)], kv.at[:, :, pl.ds(blank, HALF)],
        h_send, h_recv, {"phase": other},
    )

    def rate_of(half, i):
        rate = decay[half:half + 1, 0:1]
        for n in range(1, heads):
            rate = jnp.where(i == n, decay[half:half + 1, n:n + 1], rate)
        return jnp.broadcast_to(rate, (1, HD))

    def mix(rate):
        return jnp.where(is0, 1.0 - rate, jnp.sqrt(1.0 - rate * rate))

    def chain_head(i):
        r0, r1 = rate_of(0, i), rate_of(1, i)
        f0, f1, both = mix(r0), mix(r1), r0 * r1
        for r in range(CUTS):
            k = i * CUTS + r
            rows_at = pl.ds(r * piece, piece)
            own = kv[kept, i, tail0 + r * piece:tail0 + (r + 1) * piece, :].astype(jnp.float32)
            with scope("waittail"):
                tail_copy(k, i, r).wait_recv()
            theirs = tail_in[i, rows_at, :].astype(jnp.float32)
            low = f0 * jnp.where(is0, own, theirs)
            high = r1 * low + f1 * jnp.where(is0, theirs, own)

            @pl.when(c > 0)
            def _():
                with scope("waitchain"):
                    chain_copy(k, i, r).wait_recv()

            state = s_in[i, rows_at, :].astype(jnp.float32)
            s_out[i, rows_at, :] = (both * state + high).astype(jnp.bfloat16)

            @pl.when(c < last)
            def _():
                chain_copy(k, i, r).start()

            later = r0 * state + low
            m_out[i, rows_at, :] = jnp.where(is0, later, state).astype(jnp.bfloat16)

            @pl.when(c > 0)
            def _():
                moved_copy(k, i, r).start()

            mem[kept, i, rows_at, :] = jnp.where(is0, state, later).astype(jnp.bfloat16)

    def frame_rows():
        total = frames.shape[1]
        wide = jnp.broadcast_to(frames[...], (8, total))
        ahead = pltpu.roll(wide, HALF, 1)
        behind = pltpu.roll(wide, total - (rows - HALF), 1)
        place = lax.broadcasted_iota(jnp.int32, wide.shape, 1)
        ext = jnp.where(is0, ahead, behind)
        least = jnp.where(is0, HALF, 0)
        limit = jnp.where(is0, total + HALF, rows + HALF)
        ext = jnp.where((place >= least) & (place < limit), ext, outside_frame)
        for g in range(groups):
            fr[g] = ext[:, g * GROUP:(g + 1) * GROUP].astype(jnp.float32)

    def local_group(g):
        at = pl.ds(g * GROUP, GROUP)
        key_frame = jnp.broadcast_to(fr[g][0:1, :], (GROUP, GROUP))
        same = (
            lax.broadcasted_iota(jnp.int32, (GROUP, GROUP), 0) // WIN
            == lax.broadcasted_iota(jnp.int32, (GROUP, GROUP), 1) // WIN
        )
        allowed = same & (key_frame <= key_frame.T)
        scores = [
            lax.dot_general(
                q[i, at, :], kv[0, i, at, :],
                (((1,), (1,)), ((), ())), preferred_element_type=jnp.float32,
            )
            for i in range(heads)
        ]
        weights = [jnp.where(allowed, jnp.exp2(score * score_factor), 0.0) for score in scores]
        values = [
            jnp.dot(weights[i].astype(jnp.bfloat16), kv[1, i, at, :], preferred_element_type=jnp.float32)
            for i in range(heads)
        ]
        for i in range(heads):
            den[i, at, :] = weights[i]
            num[i, at, :] = values[i]

    spots = [(i, n * 2 * GROUP, 2 * GROUP) for i in range(heads - 1) for n in range(rows // (2 * GROUP))]
    spots += [(heads - 1, n * GROUP, GROUP) for n in range(rows // GROUP)]
    sides, crosses, relays = [], [], []
    for j, (i, first, count) in enumerate(spots):
        at = pl.ds(first, count)
        mine = att.at[me, i, at]
        sides.append(remote(mine, mine, a_send, a_recv, {"mp": sib}))
        across, passed = [], []
        for o in range(1, chips):
            to = (me + 2 * o) % n_mp
            theirs = att.at[(me + n_mp - 2 * o) % n_mp, i, at]
            across.append(remote(mine, mine, c_send, c_recv.at[j, o - 1], {"mp": to}))
            passed.append(remote(theirs, theirs, r_send, r_recv.at[max(j - len(spots) + rows // GROUP + 1, 0)], {"mp": sib}))
        crosses.append(across)
        relays.append(passed)

    direct = {}
    for n, j in enumerate(range(len(spots) - DIRECT, len(spots))):
        i, first, count = spots[j]
        mine = att.at[me, i, pl.ds(first, count)]
        direct[j] = [
            remote(mine, mine, r_send, r_recv.at[1 + rows // GROUP - DIRECT + n], {"mp": (sib + 2 * o) % n_mp})
            for o in range(1, chips)
        ]
    even = me % 2 == 0

    start = phase * (rows // WIN)

    def memory_groups(i, members):
        scores, flagged = [], []
        for g in members:
            window = start + g * (GROUP // WIN)
            row = lax.broadcasted_iota(jnp.int32, (GROUP, MEM), 0)
            flags = opened[0, window + GROUP // WIN]
            for n in range(GROUP // WIN - 1, -1, -1):
                flags = jnp.where(row < HALF + n * WIN, opened[0, window + n], flags)
            flagged.append(flags == 1)
            scores.append(lax.dot_general(
                q[i, HALF + g * GROUP:HALF + (g + 1) * GROUP, :], mem[0, i],
                (((1,), (1,)), ((), ())), preferred_element_type=jnp.float32,
            ))
        weights = [
            jnp.where(flags, jnp.exp2(score * score_factor), 0.0) for score, flags in zip(scores, flagged)
        ]
        values = [
            jnp.dot(weight.astype(jnp.bfloat16), mem[1, i], preferred_element_type=jnp.float32)
            for weight in weights
        ]
        for g, weight, value in zip(members, weights, values):
            at = slice(HALF + g * GROUP, HALF + (g + 1) * GROUP)
            total = den[i, at, :]
            for j in range(MEM // HD):
                total = total + weight[:, j * HD:(j + 1) * HD]
            denom = jnp.sum(total, axis=-1, keepdims=True)
            att[me, i, g * GROUP:(g + 1) * GROUP, :] = ((num[i, at, :] + value) / denom).astype(jnp.bfloat16)

    def memory_head(i):
        with scope("waitmem"):
            remote(m_out.at[i], mem.at[kept, i], m_send, m_recv.at[i], {"phase": other}).wait_recv()
        with scope("mem"):
            for base in range(0, rows, 2 * GROUP):
                memory_groups(i, [base // GROUP, base // GROUP + 1])
                for j, (which, first, count) in enumerate(spots):
                    if which == i and base <= first < base + 2 * GROUP:
                        for copy in crosses[j]:
                            copy.start()
                        if j in direct:
                            @pl.when(even)
                            def _(copies=direct[j]):
                                for copy in copies:
                                    copy.start()
                        sides[j].start()

    def relay_head(i, n):
        for at in range(i * per_head + n * per_head // 2, i * per_head + (n + 1) * per_head // 2):
            relay(at)

    end = heads * per_head
    plan = {}
    for kind, spots_of in enumerate(PLAN):
        for i, place in enumerate(spots_of):
            plan.setdefault(place, []).append((kind, i))

    def chain_at(place):
        if place not in plan:
            return
        kind, i = jnp.minimum(c, len(PLAN) - 1), jnp.int32(heads)
        for which, head in plan[place]:
            if head < heads:
                i = jnp.where(kind == which, head, i)

        @pl.when(i < heads)
        def _():
            with scope("chain%d" % place):
                chain_head(i)

    chain_at(0)
    with scope("head1"):
        columns(0, top, 0, wide)
    send_columns(len(wo_copies))
    chain_at(1)

    @pl.when(c == 0)
    def _():
        for r in range(CUTS):
            moved_copy(r, 0, r).start()

    with scope("head2"):
        columns(0, top, wide, 2 * wide)
    halo.start()

    chain_at(2)

    @pl.when(c == 0)
    def _():
        for i in range(1, heads):
            for r in range(CUTS):
                moved_copy(i * CUTS + r, i, r).start()

    with scope("head3"):
        columns(0, top, 2 * wide, 3 * heads)
    relay_head(0, 0)
    relay_up(0, acrosses[0])
    chain_at(3)
    with scope("local"):
        frame_rows()
        for g in range(1, groups - 1):
            local_group(g)
    relay_head(0, 1)
    chain_at(4)
    chain_at(8)
    with scope("local"):
        with scope("halo"):
            halo.wait_recv()
        local_group(0)
        local_group(groups - 1)
    relay_head(1, 0)
    chain_at(5)
    relay_head(1, 1)
    chain_at(6)
    memory_head(0)
    chain_at(7)
    relay_head(2, 0)
    memory_head(1)
    relay_head(2, 1)
    relay_up(per_head, heads * per_head)

    @pl.when(c == last)
    def _():
        for copy in wo_acrosses:
            copy.start()

    memory_head(2)

    own = pl.ds(pl.multiple_of(me * share, HD), share)

    def product(sources, which, first, count):
        left = jnp.concatenate([att[m, i, first:first + count, :] for m in sources for i in which], axis=1)
        right = jnp.concatenate([wo[m, i * HD:(i + 1) * HD, :] for m in sources for i in which], axis=0)
        return jnp.dot(left, right, preferred_element_type=jnp.float32)

    def add(sources, which, scope_name):
        with scope(scope_name):
            for first in range(0, rows, 2 * GROUP):
                at = slice(first, first + 2 * GROUP)
                acc[at, :] = acc[at, :] + product(sources, which, first, 2 * GROUP)

    def cross(j):
        for o in range(chips - 1):
            with scope("waitcross"):
                crosses[j][o].wait_recv()
            if j in direct:
                @pl.when(jnp.logical_not(even))
                def _(copy=relays[j][o]):
                    copy.start()
            else:
                relays[j][o].start()

    def arrived(lot, which):
        with scope("waitrelay"):
            remote(lot, lot, r_send, r_recv.at[which], {"mp": sib}).wait_recv()

    def far_weights(i):
        with scope("waitwo"):
            lot = wo.at[pl.ds(0, chips - 1), pl.ds(0, HD)]
            remote(lot, lot, wd_send, wr_recv.at[i], {"phase": other}).wait_recv()

            @pl.when(lazy)
            def _():
                for at in range(i * per_head, (i + 1) * per_head):
                    wo_copies[at].wait_recv()


    order = [[j for j, spot in enumerate(spots) if spot[0] == i] for i in range(heads)]
    wo_own.wait()
    with scope("own"):
        for first in range(0, rows, 2 * GROUP):
            at = slice(first, first + 2 * GROUP)
            acc[at, :] = x[at, own].astype(jnp.float32) + product([me], range(heads), first, 2 * GROUP)
    early = range(heads - 1)
    for j in order[0]:
        cross(j)
    with scope("waitside"):
        wo_side.wait_recv()
        remote(att.at[me], att.at[me], a_send, a_recv, {"mp": sib}).wait_recv()
    add([sib], range(heads), "near")
    for i in early[1:]:
        for j in order[i]:
            cross(j)
    for i in early:
        far_weights(i)
    add(far[0::2], early, "direct")
    final = order[heads - 1]
    half = len(final) // 2

    def passed():
        arrived(att.at[pl.ds(0, chips - 1), pl.ds(0, heads - 1)], 0)
        add(far[1::2], early, "passed")
        far_weights(heads - 1)

    def finish(n, size):
        first, count = spots[final[n]][1], size * spots[final[n]][2]
        for k in range(n, n + size):
            piece_at = pl.ds(spots[final[k]][1], spots[final[k]][2])
            arrived(att.at[pl.ds(0, chips - 1), heads - 1, piece_at], 1 + k)
        with scope("fin"):
            at = slice(first, first + count)
            out[at, :] = (acc[at, :] + product(far, [heads - 1], first, count)).astype(jnp.bfloat16)

    for j in final[:half]:
        cross(j)

    @pl.when(even)
    def _():
        passed()
        finish(0, half)

    for j in final[half:]:
        cross(j)

    @pl.when(even)
    def _():
        finish(half, len(final) - half)

    @pl.when(jnp.logical_not(even))
    def _():
        passed()
        finish(0, len(final))

    with scope("sends"):
        tail_all = kv.at[sent, :, pl.ds(tail0, MEM)]
        wo_all = wo.at[pl.ds(0, chips - 1)]
        att_all = att.at[pl.ds(0, chips - 1)]
        for src, send, recv, where in (
            (tail_all, y_send, y_recv.at[0], {"phase": other}),
            (m_out, m_send, m_recv.at[0], {"phase": other}),
            (wo_all, wo_send, wo_recv.at[0], {"mp": sib}),
            (att.at[me], a_send, a_recv, {"mp": sib}),
            (att_all, c_send, c_recv.at[0, 0], {"mp": sib}),
            (att_all, r_send, r_recv.at[0], {"mp": sib}),
        ):
            remote(src, src, send, recv, where).wait_send()
        halo.wait_send()
        wo_side.wait_send()

        @pl.when(c < last)
        def _():
            remote(s_out, s_in, z_send, z_recv.at[0], {"phase": other}).wait_send()

        @pl.when(c > 0)
        def _():
            remote(wo_all, wo_all, wd_send, wr_recv.at[0], {"phase": other}).wait_send()

        @pl.when(c == last - 1)
        def _():
            lot = wo.at[pl.ds(0, chips - 1), pl.ds(0, cols - block)]
            remote(lot, lot, wu_send, wr_recv.at[0], {"phase": other}).wait_send()

        @pl.when(c == last)
        def _():
            lot = wo.at[pl.ds(0, chips - 1), pl.ds(0, block)]
            remote(lot, lot, wu_send, wr_recv.at[0], {"phase": other}).wait_send()


def local(n_span, n_mp, latents, w_qkv, w_out, decay, frame_ids, memory_mask):
    rows, width = latents.shape
    cols = w_qkv.shape[2]
    heads = cols // HD
    share = width // n_mp
    ext = -(-(rows + WIN) // GROUP) * GROUP
    groups = ext // GROUP
    others = max(n_mp // 2 - 1, 1)
    chunks = 2 * others * heads
    pieces = heads * CUTS
    spots = (heads - 1) * (rows // (2 * GROUP)) + rows // GROUP
    hbm_spec = pl.BlockSpec(memory_space=pltpu.HBM)
    dma = pltpu.SemaphoreType.DMA
    bf16, f32 = jnp.bfloat16, jnp.float32
    flops = 2 * rows * width * 4 * cols
    inputs = (
        latents, jnp.transpose(w_qkv, (1, 0, 2)), w_out,
        decay.reshape(decay.shape[1:]), frame_ids, memory_mask,
    )
    return pl.pallas_call(
        functools.partial(body, (n_span, n_mp, rows, width, cols)),
        out_shape=jax.ShapeDtypeStruct((rows, share), bf16),
        in_specs=[hbm_spec] * 6,
        out_specs=pl.BlockSpec(memory_space=pltpu.VMEM),
        scratch_shapes=[
            pltpu.VMEM(decay.shape[1:], f32),
            pltpu.VMEM(frame_ids.shape, jnp.int32),
            pltpu.SMEM(memory_mask.shape, jnp.int32),
            pltpu.VMEM((rows, width), bf16),
            pltpu.VMEM((width, 3 * cols), bf16),
            pltpu.VMEM((n_mp, cols, share), bf16),
            pltpu.VMEM((2, heads, ext, HD), bf16),
            pltpu.VMEM((heads, ext, HD), bf16),
            pltpu.VMEM((heads, ext, HD), f32),
            pltpu.VMEM((heads, ext, HD), f32),
            pltpu.VMEM((n_mp, heads, rows, HD), bf16),
            pltpu.VMEM((rows, share), f32),
            pltpu.VMEM((groups, 8, GROUP), f32),
            pltpu.VMEM((heads, MEM, HD), bf16),
            pltpu.VMEM((heads, MEM, HD), bf16),
            pltpu.VMEM((heads, MEM, HD), bf16),
            pltpu.VMEM((heads, MEM, HD), bf16),
            pltpu.VMEM((2, heads, MEM, HD), bf16),
            dma((ROW_PARTS + 7,)),
            dma, dma,
            dma, dma((chunks,)), dma, dma, dma((heads,)),
            dma, dma((pieces,)),
            dma, dma((pieces,)),
            dma, dma((heads,)),
            dma, dma,
            dma, dma,
            dma, dma((spots, others)),
            dma, dma((1 + rows // GROUP,)),
        ],
        compiler_params=pltpu.CompilerParams(
            collective_id=0, has_side_effects=True, vmem_limit_bytes=40 * 1024 * 1024
        ),
        cost_estimate=pl.CostEstimate(flops=flops, bytes_accessed=12 << 20, transcendentals=1 << 20),
        name="refiner",
    )(*[pltpu.with_memory_space_constraint(a, pltpu.HBM) for a in inputs])


def solution(mesh):
    return jax.shard_map(
        functools.partial(local, mesh.shape["span"], mesh.shape["mp"]),
        mesh=mesh,
        in_specs=(
            P(("span", "phase"), None),
            P(None, None, "mp"),
            P("mp", None),
            P("span", None, "mp"),
            P("span", None),
            P("span", None),
        ),
        out_specs=P(("span", "phase"), "mp"),
        check_vma=False,
    )
```
